256 devices in a mesh: chan: 128 (over x, z_hi, y, core), tm: 2 (over z_lo).
Axes of the slice: x: 4, y: 4, z: 8 (z_hi: 4, z_lo: 2; z = z_hi * 2 + z_lo), core: 2. Of those that a mesh axis runs over, the one named last changes fastest.
Arguments:
- traces: bfloat16 [4096, 4, 2048], P('chan', None, 'tm'), may hold values from -40 to 40
- delays: int32 [1024, 4096], P(None, 'chan'), may hold values from 0 to 1023
- offsets: int32 [4], P('tm'), may hold values from 0 to 2047
Outputs:
- brightness: float32 [4, 1024, 256], P('tm', 'chan')
The draws below stay inside these ranges and needn't reach their ends.
All inputs are finite; a program needn't handle non-finite values.
Results may differ from the reference program's by a relative error of at most 0.0048.
Values may be sent and summed in bfloat16 or wider, within the bound.
No kernel may reach another device: no remote copies, remote signals or barrier semaphores. Data moves between devices by JAX's collectives and lax.ppermute only.
A program may use at most 64 MiB of HBM per device.

```python
import math
import jax
import jax.numpy as jnp
from jax import lax

CH_DEV = 32
WINDOWS = 4
NODES_DEV = 8
SAMPLES = 2048
BAND = 512
FB = 128
TB = 256
BAND_LO = 128
DEC = 8
CHANNELS = 4096
NODES = 1024
N_CHAN = 128


def draw_traces(key, part):
    keys = jax.random.split(jax.random.fold_in(key, 17), 3)
    block_len = SAMPLES // 8
    channel_scale = jnp.exp(jax.random.uniform(keys[0], (CHANNELS, 1, 1, 1), jnp.float32) * math.log(10.0))
    block_scale = jnp.exp(jax.random.uniform(keys[1], (CHANNELS, WINDOWS, 8, 1), jnp.float32) * math.log(10.0))
    noise = jnp.clip(jax.random.normal(keys[2], (CHANNELS, WINDOWS, 8, block_len), jnp.float32), -4.0, 4.0)
    values = noise * block_scale * channel_scale / 10.0
    return values.reshape(CHANNELS, WINDOWS, SAMPLES).astype(jnp.bfloat16)


def set_ends(result, own_key, low, high):
    extent = result.shape
    index_at = [jax.random.randint(jax.random.fold_in(own_key, axis), (), 0, extent[axis]) for axis in range(len(extent))]
    result = result.at[tuple(index_at)].set(low)
    longest = extent.index(max(extent))
    index_at[longest] = (index_at[longest] + 1) % extent[longest]
    return result.at[tuple(index_at)].set(high)


def setup_inputs(seed: int = 0) -> dict:
    splits = jax.random.split(jax.random.key(seed), 4)
    return {
        "traces": draw_traces(jax.random.fold_in(splits[3], 71), 0),
        "delays": set_ends(jax.random.randint(splits[1], (NODES, CHANNELS), 0, SAMPLES // 2), jax.random.fold_in(splits[1], 1), 0, (SAMPLES // 2) - 1).astype(jnp.int32),
        "offsets": set_ends(jax.random.randint(splits[2], (WINDOWS,), 0, SAMPLES), jax.random.fold_in(splits[2], 1), 0, SAMPLES - 1).astype(jnp.int32),
    }


epsilon = 1e-06
full_turn = 2.0 * math.pi

def angle_grid(first_ids, second_ids):
    product = first_ids[:, None] * second_ids[None, :] % SAMPLES
    return product.astype(jnp.float32) * (full_turn / SAMPLES)

def reference(traces, delays, offsets):
    sample_ids = jnp.arange(SAMPLES, dtype=jnp.int32)
    band_bins = BAND_LO + jnp.arange(BAND, dtype=jnp.int32)
    taper = jnp.sin(jnp.pi * (jnp.arange(BAND, dtype=jnp.float32) + 0.5) / BAND) ** 2
    forward_angles = angle_grid(sample_ids, band_bins)
    forward = jnp.concatenate([jnp.cos(forward_angles), -jnp.sin(forward_angles)], axis=1).astype(jnp.bfloat16)
    back_angles = angle_grid(band_bins, sample_ids)
    weight = (2.0 * taper / SAMPLES)[:, None]
    upper = jnp.concatenate([weight * jnp.cos(back_angles), weight * jnp.sin(back_angles)], axis=1)
    lower = jnp.concatenate([-weight * jnp.sin(back_angles), weight * jnp.cos(back_angles)], axis=1)
    inverse = jnp.concatenate([upper, lower], axis=0).astype(jnp.bfloat16)
    env_bins = 1 + jnp.arange(FB, dtype=jnp.int32)
    env_angles = angle_grid(sample_ids, env_bins)
    envelope_table = jnp.concatenate([jnp.cos(env_angles), -jnp.sin(env_angles)], axis=1).astype(jnp.bfloat16)

    def process(block_traces):
        trace_rows = block_traces.reshape(CH_DEV * WINDOWS, SAMPLES)
        spectrum = jnp.dot(trace_rows, forward, preferred_element_type=jnp.float32).astype(jnp.bfloat16)
        analytic = jnp.dot(spectrum, inverse, preferred_element_type=jnp.float32)
        real_part = analytic[:, :SAMPLES]
        imag_part = analytic[:, SAMPLES:]
        energy = real_part * real_part + imag_part * imag_part
        energy_sum = lax.optimization_barrier(jnp.sum(energy, axis=1))
        envelope_spectrum = jnp.dot(energy.astype(jnp.bfloat16), envelope_table, preferred_element_type=jnp.float32)
        factor = 1.0 / (math.sqrt(SAMPLES) * (energy_sum / SAMPLES + epsilon))
        normalized = (envelope_spectrum * factor[:, None]).astype(jnp.bfloat16)
        return normalized.reshape(CH_DEV, WINDOWS, 2 * FB)
    normalized = lax.map(process, traces.reshape(N_CHAN, CH_DEV, WINDOWS, SAMPLES))
    normalized = normalized.reshape(CHANNELS, WINDOWS, 2 * FB)
    e_real = normalized[:, :, :FB]
    e_imag = normalized[:, :, FB:]
    real_block = jnp.concatenate([e_real, -e_imag], axis=0)
    imag_block = jnp.concatenate([e_imag, e_real], axis=0)
    spectra_pair = jnp.concatenate([real_block, imag_block], axis=1).astype(jnp.float32)

    def stack_block(delay_rows):
        product = delay_rows[:, :, None] * env_bins[None, None, :] % SAMPLES
        angles = product.astype(jnp.float32) * (full_turn / SAMPLES)
        phase = jnp.concatenate([jnp.cos(angles), jnp.sin(angles)], axis=1).astype(jnp.bfloat16)
        return jnp.einsum('ncf,cwf->nwf', phase.astype(jnp.float32), spectra_pair)
    stacks = lax.map(stack_block, delays.reshape(N_CHAN, NODES_DEV, CHANNELS))
    stacks = stacks.reshape(NODES, 2, WINDOWS, FB)
    out_times = offsets[:, None] + DEC * jnp.arange(TB, dtype=jnp.int32)[None, :]
    product = env_bins[None, :, None] * out_times[:, None, :] % SAMPLES
    out_angles = product.astype(jnp.float32) * (full_turn / SAMPLES)
    scale = 1.0 / math.sqrt(FB * CHANNELS)
    bright = jnp.einsum('nwf,wfk->wnk', stacks[:, 0], jnp.cos(out_angles), precision=lax.Precision.HIGHEST)
    bright = bright - jnp.einsum('nwf,wfk->wnk', stacks[:, 1], jnp.sin(out_angles), precision=lax.Precision.HIGHEST)
    return bright * scale
```

```python
import math

import jax
import jax.numpy as jnp
import numpy as np
from jax import lax
from jax.experimental import pallas as pl
from jax.experimental.pallas import tpu as pltpu
from jax.sharding import Mesh
from jax.sharding import PartitionSpec as P

SAMPLES = 2048
HALF = 1024
BAND = 512
FB = 128
TB = 256
BAND_LO = 128
DEC = 8
CHANNELS = 4096
epsilon = 1e-06
bf16 = jnp.bfloat16
f32 = jnp.float32
VMEM = pl.BlockSpec(memory_space=pltpu.VMEM)
SMEM = pl.BlockSpec(memory_space=pltpu.SMEM)


def tables():
    t = np.arange(HALF)
    k = BAND_LO + np.arange(BAND)
    taper = np.sin(np.pi * (np.arange(BAND) + 0.5) / BAND) ** 2
    g = (2.0 * taper / SAMPLES)[:, None]
    turn = 2.0 * np.pi / SAMPLES
    a = (t[:, None] * k[None, :] % SAMPLES) * turn
    forward = np.concatenate([np.cos(a), -np.sin(a)], axis=1).astype(np.float32)
    b = a.T
    upper = np.concatenate([g * np.cos(b), g * np.sin(b)], axis=1)
    lower = np.concatenate([-g * np.sin(b), g * np.cos(b)], axis=1)
    inverse = np.concatenate([upper, lower], axis=0).astype(np.float32)
    f = 1 + np.arange(FB)
    e = (t[:, None] * f[None, :] % SAMPLES) * turn
    envelope = np.concatenate([np.cos(e), -np.sin(e)], axis=1).astype(np.float32)
    o = (f[:, None] * (DEC * np.arange(TB))[None, :] % SAMPLES) * turn
    times = np.stack([np.cos(o), np.sin(o)]).astype(np.float32)
    low = lambda v: v.astype(bf16)
    return low(forward), low(inverse), low(envelope), times


def half_turn(u):
    v = u * u
    s = 1.0 + v * (-1 / 6 + v * (1 / 120 + v * (-1 / 5040 + v * (1 / 362880 + v * (-1 / 39916800)))))
    c = 1.0 + v * (
        -1 / 2 + v * (1 / 24 + v * (-1 / 720 + v * (1 / 40320 + v * (-1 / 3628800 + v * (1 / 479001600)))))
    )
    return -(u * s), c


def prep_kernel(ids, offs, d_ref, times_ref, d0, d1, d2, d3, q_ref, rows):
    zh, core = ids[1], ids[2]
    for m in range(8):
        rows[pl.ds(128 * m, 128), :] = d_ref[:, pl.ds(128 * m, 128)].astype(f32).T
    for k, out in enumerate((d0, d1, d2, d3)):
        to_zh = (zh + k) & 3
        for b in range(2):
            to_core = core ^ b
            parts = []
            for x in range(4):
                for y in range(4):
                    at = pl.multiple_of((((x * 4 + to_zh) * 4 + y) * 2 + to_core) * 8, 8)
                    parts.append(rows[pl.ds(at, 8), :])
            out[b] = jnp.concatenate(parts, axis=0).T.astype(jnp.int32)
    scale = 1.0 / math.sqrt(FB * CHANNELS)
    f = 1 + lax.broadcasted_iota(jnp.int32, (FB, TB), 0)
    for w in range(2):
        p = (f * offs[w]) & (SAMPLES - 1)
        c, s = half_turn((p - HALF).astype(f32) * (math.pi / SAMPLES))
        c, s = c * c - s * s, 2.0 * c * s
        q_ref[w, :FB] = (times_ref[0] * c - times_ref[1] * s) * scale
        q_ref[w, FB:] = (times_ref[1] * c + times_ref[0] * s) * -scale


def front_kernel(ids, own_ref, peer_ref, fwd_ref, inv_ref, env_ref, e_ref):
    tm = ids[3]
    own = own_ref[pl.ds(2 * tm, 2)].reshape(64, HALF)
    peer = peer_ref[...].reshape(64, HALF)
    terms = jnp.dot(jnp.concatenate([own, peer], axis=0), fwd_ref[...], preferred_element_type=f32)
    col = lax.broadcasted_iota(jnp.int32, (1, 2 * BAND), 1)
    sign = (1 - 2 * (col & 1)).astype(f32)
    first = jnp.where(tm == 0, jnp.ones_like(sign), sign)
    second = jnp.where(tm == 0, sign, jnp.ones_like(sign))
    spectrum = terms[:64] * first + terms[64:] * second
    both = jnp.concatenate([spectrum, spectrum * sign], axis=0).astype(bf16)
    analytic = jnp.dot(both, inv_ref[...], preferred_element_type=f32)
    real, imag = analytic[:, :HALF], analytic[:, HALF:]
    energy = real * real + imag * imag
    sums = jnp.sum(energy, axis=1, keepdims=True)
    sums = sums[:64] + sums[64:]
    env = jnp.dot(energy.astype(bf16), env_ref[...], preferred_element_type=f32)
    lane = lax.broadcasted_iota(jnp.int32, (1, 2 * FB), 1)
    odd = (2 * (lane & 1) - 1).astype(f32)
    env = env[:64] + env[64:] * odd
    factor = 1.0 / (math.sqrt(SAMPLES) * (sums / SAMPLES + epsilon))
    e_ref[...] = (env * factor).astype(bf16)


def phase_kernel(r0, r1, r2, r3, x_ref, z_ref):
    for k, r in enumerate((r0, r1, r2, r3)):
        for b in range(2):
            d = r[0] if b == 0 else x_ref[k]
            c1, s1 = half_turn((d - 512).astype(f32) * (math.pi / 1024))
            at = 64 * k + 32 * b

            def step(f, state):
                c, s = state
                z_ref[f, pl.ds(at, 32), :] = c.astype(bf16)
                z_ref[f, pl.ds(256 + at, 32), :] = s.astype(bf16)
                return c * c1 - s * s1, c * s1 + s * c1

            lax.fori_loop(0, FB, step, (c1, s1), unroll=8)


def stack_kernel(e0, e1, e2, e3, z_ref, out_ref, lhs, acc):
    for w in range(2):
        rows = [e[b, pl.ds(32 * w, 32), :] for e in (e0, e1, e2, e3) for b in range(2)]
        t = jnp.concatenate(rows, axis=0).astype(f32).T
        re, im = t[:FB], t[FB:]
        q = 2 * w * FB
        for i in range(2):
            half = slice(128 * i, 128 * i + 128)
            lhs[i, pl.ds(q, FB), :] = re[:, half]
            lhs[i + 2, pl.ds(q, FB), :] = -im[:, half]
            lhs[i, pl.ds(q + FB, FB), :] = im[:, half]
            lhs[i + 2, pl.ds(q + FB, FB), :] = re[:, half]

    def step(f, _):
        a = jnp.concatenate([lhs[i, pl.ds(f, 4, stride=FB), :] for i in range(4)], axis=1)
        acc[pl.ds(f, 4, stride=FB), :] = jnp.dot(a.astype(bf16), z_ref[f], preferred_element_type=f32)
        return 0

    lax.fori_loop(0, FB, step, 0, unroll=8)
    out_ref[...] = acc[...].T.astype(bf16)


def final_kernel(part_ref, q_ref, out_ref):
    total = part_ref[0:16, :].astype(f32)
    for i in range(1, 8):
        total = total + part_ref[16 * i : 16 * i + 16, :].astype(f32)
    total = total[:8] + total[8:]
    for w in range(2):
        out_ref[w] = jnp.dot(
            total[:, w * TB : (w + 1) * TB], q_ref[w], precision=lax.Precision.HIGHEST, preferred_element_type=f32
        )


def call(kernel, outs, n_smem, n_vmem, scratch=()):
    return pl.pallas_call(
        kernel,
        out_shape=outs,
        in_specs=[SMEM] * n_smem + [VMEM] * n_vmem,
        out_specs=jax.tree.map(lambda _: VMEM, outs),
        scratch_shapes=list(scratch),
        compiler_params=pltpu.CompilerParams(vmem_limit_bytes=40 << 20),
    )


def shift(v, axis, k):
    n = lax.axis_size(axis)
    return lax.ppermute(v, axis, [(i, (i + k) % n) for i in range(n)])


def shape(dims, dtype):
    return jax.ShapeDtypeStruct(dims, dtype)


def make(consts):
    forward, inverse, envelope, times = consts

    def on_device(traces, delays, offsets):
        tm = lax.axis_index("tm")
        ids = jnp.stack([lax.axis_index(a) for a in ("x", "zh", "core", "tm")]).astype(jnp.int32)
        rows = traces.transpose(1, 0, 2)
        send = jnp.where(tm == 0, rows[2:], rows[:2])
        peer = shift(send, "tm", 1)
        piece = shape((2, 32, 128), jnp.int32)
        d0, d1, d2, d3, q = call(
            prep_kernel,
            (piece, piece, piece, piece, shape((2, 2 * FB, TB), f32)),
            2,
            2,
            [pltpu.VMEM((1024, 32), f32)],
        )(ids, offsets, delays.T, jnp.asarray(times))
        r = [d0] + [shift(v, "zh", k) for k, v in ((1, d1), (2, d2), (3, d3))]
        x = shift(jnp.stack([v[1] for v in r]), "core", 1)
        e = call(front_kernel, shape((64, 2 * FB), bf16), 1, 5)(
            ids, rows, peer, jnp.asarray(forward), jnp.asarray(inverse), jnp.asarray(envelope)
        )
        r, x, e = lax.optimization_barrier((r, x, e))
        pair = jnp.stack([e, shift(e, "core", 1)])
        pairs = [pair] + [shift(pair, "zh", k) for k in (1, 2, 3)]
        z = call(phase_kernel, shape((FB, 512, 128), bf16), 0, 5)(*r, x)
        part = call(
            stack_kernel,
            shape((128, 512), bf16),
            0,
            5,
            [pltpu.VMEM((4, 512, 128), f32), pltpu.VMEM((512, 128), f32)],
        )(*pairs, z)
        parts = lax.all_to_all(part.reshape(16, 8, 512), ("x", "y"), 0, 0, tiled=True)
        return call(final_kernel, shape((2, 8, TB), f32), 0, 2)(parts.reshape(128, 512), q)

    return on_device


def solution(mesh):
    chan = ("x", "zh", "y", "core")
    fine = Mesh(mesh.devices.reshape(4, 4, 4, 2, 2), chan + ("tm",))
    placed = (P(chan, None, "tm"), P(None, chan), P("tm"))
    return jax.shard_map(
        make(tables()), mesh=fine, in_specs=placed, out_specs=P("tm", chan, None), check_vma=False
    )
```

```python
import functools
import math

import jax
import jax.numpy as jnp
from jax import lax
from jax.experimental import pallas as pl
from jax.experimental.pallas import tpu as pltpu
from jax.sharding import Mesh
from jax.sharding import PartitionSpec as P

SAMPLES = 2048
HALF = 1024
BAND = 512
FB = 128
TB = 256
BAND_LO = 128
DEC = 8
CHANNELS = 4096
epsilon = 1e-06
bf16 = jnp.bfloat16
f32 = jnp.float32
VMEM = pl.BlockSpec(memory_space=pltpu.VMEM)
SMEM = pl.BlockSpec(memory_space=pltpu.SMEM)


def half_turn(u):
    v = u * u
    s = 1.0 + v * (-1 / 6 + v * (1 / 120 + v * (-1 / 5040 + v * (1 / 362880 + v * (-1 / 39916800)))))
    c = 1.0 + v * (
        -1 / 2 + v * (1 / 24 + v * (-1 / 720 + v * (1 / 40320 + v * (-1 / 3628800 + v * (1 / 479001600)))))
    )
    return -(u * s), c


def circle(p):
    c, s = half_turn(((p & (SAMPLES - 1)) - HALF).astype(f32) * (math.pi / SAMPLES))
    return c * c - s * s, 2.0 * c * s


def iota(dims, axis):
    return lax.broadcasted_iota(jnp.int32, dims, axis)


def prep_kernel(ids, offs, d_ref, mine, send, q_ref, fwd_ref, inv_ref, env_ref, rows, base):
    zh, core = ids[1], ids[2]
    for m in range(8):
        rows[pl.ds(128 * m, 128), :] = d_ref[:, pl.ds(128 * m, 128)].astype(f32).T
    for k in range(4):
        to_zh = (zh + k) & 3
        for b, out in enumerate((mine, send)):
            to_core = core ^ b
            parts = []
            for x in range(4):
                for y in range(4):
                    at = pl.multiple_of((((x * 4 + to_zh) * 4 + y) * 2 + to_core) * 8, 8)
                    parts.append(rows[pl.ds(at, 8), :])
            out[k] = jnp.concatenate(parts, axis=0).T.astype(jnp.int32)
    scale = 1.0 / math.sqrt(FB * CHANNELS)
    for w in range(2):
        c, s = circle((1 + iota((FB, TB), 0)) * (DEC * iota((FB, TB), 1) + offs[w]))
        q_ref[w, :FB] = c * scale
        q_ref[w, FB:] = s * -scale
    wide = BAND + FB
    lane = iota((32, wide), 1)
    freq = jnp.where(lane < BAND, BAND_LO + lane, lane - BAND + 1)
    step = iota((32, wide), 0) * freq
    base[0], base[1] = circle(32 * step)
    cb, sb = circle(step)
    _, taper = circle(2 * iota((1, BAND), 1) + 1)
    weight = taper * taper * (2.0 / SAMPLES)

    def body(a, _):
        ca, sa = base[0, pl.ds(a, 1), :], base[1, pl.ds(a, 1), :]
        c, s = ca * cb - sa * sb, sa * cb + ca * sb
        at = pl.ds(pl.multiple_of(32 * a, 32), 32)
        fwd_ref[at, :BAND] = c[:, :BAND].astype(bf16)
        fwd_ref[at, BAND:] = (-s[:, :BAND]).astype(bf16)
        inv_ref[at, :BAND] = (weight * c[:, :BAND]).astype(bf16)
        inv_ref[at, BAND:] = (weight * s[:, :BAND]).astype(bf16)
        env_ref[at, :FB] = c[:, BAND:].astype(bf16)
        env_ref[at, FB:] = (-s[:, BAND:]).astype(bf16)
        return 0

    lax.fori_loop(0, 32, body, 0)


def front_kernel(ids, own_ref, peer_ref, fwd_ref, inv_ref, env_ref, lhs_ref, lhs):
    tm = ids[3]
    own = own_ref[pl.ds(2 * tm, 2)].reshape(64, HALF)
    peer = peer_ref[...].reshape(64, HALF)
    terms = jnp.dot(jnp.concatenate([own, peer], axis=0), fwd_ref[...], preferred_element_type=f32)
    col = lax.broadcasted_iota(jnp.int32, (1, 2 * BAND), 1)
    sign = (1 - 2 * (col & 1)).astype(f32)
    first = jnp.where(tm == 0, jnp.ones_like(sign), sign)
    second = jnp.where(tm == 0, sign, jnp.ones_like(sign))
    spectrum = terms[:64] * first + terms[64:] * second
    both = jnp.concatenate([spectrum, spectrum * sign], axis=0)
    re, im = both[:, :BAND], both[:, BAND:]
    real_form = jnp.concatenate([re, -im], axis=1)
    imag_form = jnp.concatenate([im, re], axis=1)
    forms = jnp.concatenate([real_form, imag_form], axis=0).astype(bf16)
    analytic = lax.dot_general(forms, inv_ref[...], (((1,), (1,)), ((), ())), preferred_element_type=f32)
    real, imag = analytic[:128], analytic[128:]
    energy = real * real + imag * imag
    sums = jnp.sum(energy, axis=1, keepdims=True)
    sums = sums[:64] + sums[64:]
    env = jnp.dot(energy.astype(bf16), env_ref[...], preferred_element_type=f32)
    lane = lax.broadcasted_iota(jnp.int32, (1, 2 * FB), 1)
    odd = (2 * (lane & 1) - 1).astype(f32)
    env = env[:64] + env[64:] * odd
    factor = 1.0 / (math.sqrt(SAMPLES) * (sums / SAMPLES + epsilon))
    normal = (env * factor).astype(bf16).astype(f32)
    freq = lax.broadcasted_iota(jnp.int32, (FB, 128), 0)
    lanes = lax.broadcasted_iota(jnp.int32, (FB, 128), 1)
    kept = (freq & 1) == (lanes >> 6)
    for w in range(2):
        re = normal[32 * w : 32 * w + 32, :FB]
        im = normal[32 * w : 32 * w + 32, FB:]
        for part, quad in enumerate(((re, -im, re, -im), (im, re, im, re))):
            t = jnp.concatenate(quad, axis=0).T
            lhs[pl.ds(2 * w + part, FB, stride=4), :] = jnp.where(kept, t, 0.0)
    lhs_ref[...] = lhs[...].astype(bf16)


def chunk_kernel(k, own_d, other_d, own_lhs, other_lhs, out_ref, acc):
    steps = []
    for d in (own_d, other_d):
        steps.append(half_turn((d[k] - 512).astype(f32) * (math.pi / 1024)))

    def turn(state):
        return [(c * a - s * b, c * b + s * a) for (c, s), (a, b) in zip(state, steps)]

    def body(i, state):
        at = pl.multiple_of(16 * i, 16)
        a = jnp.concatenate([own_lhs[pl.ds(at, 16), :], other_lhs[pl.ds(at, 16), :]], axis=1)
        for g in range(2):
            odd = turn(state)
            z = [v.astype(bf16) for e, o in zip(state, odd) for v in (*e, *o)]
            r = jnp.dot(a, jnp.concatenate(z, axis=0), preferred_element_type=f32)
            acc[pl.ds(at + 8 * g, 8), :] = r[8 * g : 8 * g + 8]
            state = turn(odd)
        return state

    lax.fori_loop(0, FB // 4, body, steps, unroll=2)
    for q in range(4):
        out_ref[:, 128 * q : 128 * q + 128] = acc[pl.ds(q, FB, stride=4), :].T.astype(bf16)


def final_kernel(part_ref, q_ref, out_ref):
    total = part_ref[0:16, :].astype(f32)
    for i in range(1, 8):
        total = total + part_ref[16 * i : 16 * i + 16, :].astype(f32)
    total = total[:8] + total[8:]
    for w in range(2):
        out_ref[w] = jnp.dot(
            total[:, w * TB : (w + 1) * TB], q_ref[w], precision=lax.Precision.HIGHEST, preferred_element_type=f32
        )


def call(kernel, outs, ins, scratch=(), limit=24, cost=None):
    return pl.pallas_call(
        kernel,
        out_shape=outs,
        in_specs=ins,
        out_specs=jax.tree.map(lambda _: VMEM, outs),
        scratch_shapes=list(scratch),
        cost_estimate=cost,
        compiler_params=pltpu.CompilerParams(vmem_limit_bytes=limit << 20),
    )


def shift(v, axis, k):
    n = lax.axis_size(axis)
    return lax.ppermute(v, axis, [(i, (i + k) % n) for i in range(n)])


def shape(dims, dtype):
    return jax.ShapeDtypeStruct(dims, dtype)


def on_device(traces, delays, offsets):
    tm = lax.axis_index("tm")
    ids = jnp.stack([lax.axis_index(a) for a in ("x", "zh", "core", "tm")]).astype(jnp.int32)
    rows = traces.transpose(1, 0, 2)
    send = jnp.where(tm == 0, rows[2:], rows[:2])
    send, offsets, ids = lax.optimization_barrier((send, offsets, ids))
    peer = shift(send, "tm", 1)
    nodes = shape((4, 32, 128), jnp.int32)
    mine, theirs, q, fwd, inv, env = call(
        prep_kernel,
        (
            nodes,
            nodes,
            shape((2, 2 * FB, TB), f32),
            shape((HALF, 2 * BAND), bf16),
            shape((HALF, 2 * BAND), bf16),
            shape((HALF, 2 * FB), bf16),
        ),
        [SMEM, SMEM, VMEM],
        [pltpu.VMEM((1024, 32), f32), pltpu.VMEM((2, 32, BAND + FB), f32)],
    )(ids, offsets, delays.T)
    other = shift(theirs, "core", 1)
    lhs = call(
        front_kernel, shape((512, 128), bf16), [SMEM] + [VMEM] * 5, [pltpu.VMEM((512, 128), f32)]
    )(ids, rows, peer, fwd, inv, env)
    lhs_other = shift(lhs, "core", 1)
    got = []
    for k in (1, 2, 3, 0):
        part = call(
            functools.partial(chunk_kernel, k),
            shape((128, 512), bf16),
            [VMEM] * 4,
            [pltpu.VMEM((512, 128), f32)],
            cost=pl.CostEstimate(flops=1000, transcendentals=0, bytes_accessed=1000),
        )(mine, other, lhs, lhs_other)
        lhs, part = lax.optimization_barrier((lhs, part))
        got.append(part if k == 0 else shift(part, "zh", k))
    part = sum(v.astype(f32) for v in got).astype(bf16)
    parts = lax.all_to_all(part.reshape(16, 8, 512), ("x", "y"), 0, 0, tiled=True)
    return call(final_kernel, shape((2, 8, TB), f32), [VMEM] * 2)(parts.reshape(128, 512), q)


def solution(mesh):
    chan = ("x", "zh", "y", "core")
    fine = Mesh(mesh.devices.reshape(4, 4, 4, 2, 2), chan + ("tm",))
    placed = (P(chan, None, "tm"), P(None, chan), P("tm"))
    return jax.shard_map(
        on_device, mesh=fine, in_specs=placed, out_specs=P("tm", chan, None), check_vma=False
    )
```

```python
import functools
import math

import jax
import jax.numpy as jnp
from jax import lax
from jax.experimental import pallas as pl
from jax.experimental.pallas import tpu as pltpu
from jax.sharding import Mesh
from jax.sharding import PartitionSpec as P

SAMPLES = 2048
HALF = 1024
BAND = 512
FB = 128
TB = 256
BAND_LO = 128
DEC = 8
CHANNELS = 4096
epsilon = 1e-06
bf16 = jnp.bfloat16
f32 = jnp.float32
VMEM = pl.BlockSpec(memory_space=pltpu.VMEM)
SMEM = pl.BlockSpec(memory_space=pltpu.SMEM)


def half_turn(u):
    v = u * u
    s = 1.0 + v * (-1 / 6 + v * (1 / 120 + v * (-1 / 5040 + v * (1 / 362880 + v * (-1 / 39916800)))))
    c = 1.0 + v * (
        -1 / 2 + v * (1 / 24 + v * (-1 / 720 + v * (1 / 40320 + v * (-1 / 3628800 + v * (1 / 479001600)))))
    )
    return -(u * s), c


def circle(p):
    c, s = half_turn(((p & (SAMPLES - 1)) - HALF).astype(f32) * (math.pi / SAMPLES))
    return c * c - s * s, 2.0 * c * s


def iota(dims, axis):
    return lax.broadcasted_iota(jnp.int32, dims, axis)


def delay_kernel(ids, d_ref, mine, send, rows):
    x, core = ids[0], ids[2]
    for m in range(8):
        rows[pl.ds(128 * m, 128), :] = d_ref[:, pl.ds(128 * m, 128)].astype(f32).T
    for k in range(4):
        to_x = (x + k) & 3
        for b, out in enumerate((mine, send)):
            to_core = core ^ b
            parts = []
            for zy in range(16):
                at = pl.multiple_of(((to_x * 16 + zy) * 2 + to_core) * 8, 8)
                parts.append(rows[pl.ds(at, 8), :])
            out[k] = jnp.concatenate(parts, axis=0).T.astype(jnp.int32)


def table_kernel(ids, after, q_ref, fwd_ref, inv_ref, env_ref, base):
    scale = 1.0 / math.sqrt(FB * CHANNELS)
    for w in range(2):
        c, s = circle((1 + iota((FB, TB), 0)) * (DEC * iota((FB, TB), 1) + ids[4 + w]))
        q_ref[w, :FB] = c * scale
        q_ref[w, FB:] = s * -scale
    wide = BAND + FB
    lane = iota((32, wide), 1)
    freq = jnp.where(lane < BAND, BAND_LO + lane, lane - BAND + 1)
    step = iota((32, wide), 0) * freq
    base[0], base[1] = circle(32 * step)
    cb, sb = circle(step)
    _, taper = circle(2 * iota((1, BAND), 1) + 1)
    weight = taper * taper * (2.0 / SAMPLES)

    def body(a, _):
        ca, sa = base[0, pl.ds(a, 1), :], base[1, pl.ds(a, 1), :]
        c, s = ca * cb - sa * sb, sa * cb + ca * sb
        at = pl.ds(pl.multiple_of(32 * a, 32), 32)
        fwd_ref[at, :BAND] = c[:, :BAND].astype(bf16)
        fwd_ref[at, BAND:] = (-s[:, :BAND]).astype(bf16)
        inv_ref[at, :BAND] = (weight * c[:, :BAND]).astype(bf16)
        inv_ref[at, BAND:] = (weight * s[:, :BAND]).astype(bf16)
        env_ref[at, :FB] = c[:, BAND:].astype(bf16)
        env_ref[at, FB:] = (-s[:, BAND:]).astype(bf16)
        return 0

    lax.fori_loop(0, 32, body, 0)


def front_kernel(ids, own_ref, peer_ref, fwd_ref, inv_ref, env_ref, lhs_ref, lhs):
    tm = ids[3]
    own = own_ref[pl.ds(2 * tm, 2)].reshape(64, HALF)
    peer = peer_ref[...].reshape(64, HALF)
    terms = jnp.dot(jnp.concatenate([own, peer], axis=0), fwd_ref[...], preferred_element_type=f32)
    col = lax.broadcasted_iota(jnp.int32, (1, 2 * BAND), 1)
    sign = (1 - 2 * (col & 1)).astype(f32)
    first = jnp.where(tm == 0, jnp.ones_like(sign), sign)
    second = jnp.where(tm == 0, sign, jnp.ones_like(sign))
    spectrum = terms[:64] * first + terms[64:] * second
    both = jnp.concatenate([spectrum, spectrum * sign], axis=0)
    re, im = both[:, :BAND], both[:, BAND:]
    real_form = jnp.concatenate([re, -im], axis=1)
    imag_form = jnp.concatenate([im, re], axis=1)
    forms = jnp.concatenate([real_form, imag_form], axis=0).astype(bf16)
    analytic = lax.dot_general(forms, inv_ref[...], (((1,), (1,)), ((), ())), preferred_element_type=f32)
    real, imag = analytic[:128], analytic[128:]
    energy = real * real + imag * imag
    sums = jnp.sum(energy, axis=1, keepdims=True)
    sums = sums[:64] + sums[64:]
    env = jnp.dot(energy.astype(bf16), env_ref[...], preferred_element_type=f32)
    lane = lax.broadcasted_iota(jnp.int32, (1, 2 * FB), 1)
    odd = (2 * (lane & 1) - 1).astype(f32)
    env = env[:64] + env[64:] * odd
    factor = 1.0 / (math.sqrt(SAMPLES) * (sums / SAMPLES + epsilon))
    normal = (env * factor).astype(bf16).astype(f32)
    freq = lax.broadcasted_iota(jnp.int32, (FB, 128), 0)
    lanes = lax.broadcasted_iota(jnp.int32, (FB, 128), 1)
    kept = (freq & 1) == (lanes >> 6)
    for w in range(2):
        re = normal[32 * w : 32 * w + 32, :FB]
        im = normal[32 * w : 32 * w + 32, FB:]
        for part, quad in enumerate(((re, -im, re, -im), (im, re, im, re))):
            t = jnp.concatenate(quad, axis=0).T
            lhs[pl.ds(2 * w + part, FB, stride=4), :] = jnp.where(kept, t, 0.0)
    lhs_ref[...] = lhs[...].astype(bf16)


def turn(u, v):
    return u[0] * v[0] - u[1] * v[1], u[0] * v[1] + u[1] * v[0]


def chunk_kernel(k, own_d, other_d, own_lhs, other_lhs, out_ref, acc):
    one = [half_turn((d[k] - 512).astype(f32) * (math.pi / 1024)) for d in (own_d, other_d)]
    two = [turn(v, v) for v in one]
    mid = two
    for i in range(FB // 4):
        powers, ahead = [[], [], [], []], []
        for (c, s), (c1, s1), v2 in zip(mid, one, two):
            cc, ss, cs, sc = c * c1, s * s1, c * s1, s * c1
            last = turn((c, s), v2)
            for group, v in zip(powers, ((cc + ss, sc - cs), (c, s), (cc - ss, sc + cs), last)):
                group.append([x.astype(bf16) for x in v])
            ahead.append(turn(last, v2))
        mid = ahead
        at = 16 * i
        a = jnp.concatenate([own_lhs[at : at + 16, :], other_lhs[at : at + 16, :]], axis=1)
        for g in range(2):
            z = [x for even, odd in zip(powers[2 * g], powers[2 * g + 1]) for x in (*even, *odd)]
            r = jnp.dot(a, jnp.concatenate(z, axis=0), preferred_element_type=f32)
            acc[at + 8 * g : at + 8 * g + 8, :] = r[8 * g : 8 * g + 8]
    for q in range(4):
        out_ref[:, 128 * q : 128 * q + 128] = acc[pl.ds(q, FB, stride=4), :].T.astype(bf16)


def final_kernel(part_ref, q_ref, out_ref):
    total = part_ref[0:16, :].astype(f32)
    for i in range(1, 8):
        total = total + part_ref[16 * i : 16 * i + 16, :].astype(f32)
    total = total[:8] + total[8:]
    for w in range(2):
        out_ref[w] = jnp.dot(
            total[:, w * TB : (w + 1) * TB], q_ref[w], precision=lax.Precision.HIGHEST, preferred_element_type=f32
        )


def call(kernel, outs, ins, scratch=(), limit=24):
    return pl.pallas_call(
        kernel,
        out_shape=outs,
        in_specs=ins,
        out_specs=jax.tree.map(lambda _: VMEM, outs),
        scratch_shapes=list(scratch),
        compiler_params=pltpu.CompilerParams(vmem_limit_bytes=limit << 20),
    )


def shift(v, axis, k):
    n = lax.axis_size(axis)
    return lax.ppermute(v, axis, [(i, (i + k) % n) for i in range(n)])


def shape(dims, dtype):
    return jax.ShapeDtypeStruct(dims, dtype)


def on_device(traces, delays, offsets):
    tm = lax.axis_index("tm")
    ids = jnp.stack([lax.axis_index(a) for a in ("x", "zh", "core", "tm")]).astype(jnp.int32)
    rows = traces.transpose(1, 0, 2)
    send = jnp.where(tm == 0, rows[2:], rows[:2])
    ids = jnp.concatenate([ids, offsets])
    send, ids = lax.optimization_barrier((send, ids))
    peer = shift(send, "tm", 1)
    nodes = shape((4, 32, 128), jnp.int32)
    mine, theirs = call(delay_kernel, (nodes, nodes), [SMEM, VMEM], [pltpu.VMEM((1024, 32), f32)])(ids, delays.T)
    other = shift(theirs, "core", 1)
    q, fwd, inv, env = call(
        table_kernel,
        (
            shape((2, 2 * FB, TB), f32),
            shape((HALF, 2 * BAND), bf16),
            shape((HALF, 2 * BAND), bf16),
            shape((HALF, 2 * FB), bf16),
        ),
        [SMEM, VMEM],
        [pltpu.VMEM((2, 32, BAND + FB), f32)],
    )(ids, mine)
    peer, other, fwd = lax.optimization_barrier((peer, other, fwd))
    lhs = call(
        front_kernel, shape((512, 128), bf16), [SMEM] + [VMEM] * 5, [pltpu.VMEM((512, 128), f32)]
    )(ids, rows, peer, fwd, inv, env)
    lhs_other = shift(lhs, "core", 1)
    got = []
    for k in (1, 2, 3, 0):
        part = call(
            functools.partial(chunk_kernel, k),
            shape((128, 512), bf16),
            [VMEM] * 4,
            [pltpu.VMEM((512, 128), f32)],
        )(mine, other, lhs, lhs_other)
        lhs, part = lax.optimization_barrier((lhs, part))
        got.append(part if k == 0 else shift(part, "x", k))
    part = sum(v.astype(f32) for v in got).astype(bf16)
    parts = lax.all_to_all(part.reshape(16, 8, 512), ("zh", "y"), 0, 0, tiled=True)
    return call(final_kernel, shape((2, 8, TB), f32), [VMEM] * 2)(parts.reshape(128, 512), q)


def solution(mesh):
    chan = ("x", "zh", "y", "core")
    fine = Mesh(mesh.devices.reshape(4, 4, 4, 2, 2), chan + ("tm",))
    placed = (P(chan, None, "tm"), P(None, chan), P("tm"))
    return jax.shard_map(
        on_device, mesh=fine, in_specs=placed, out_specs=P("tm", chan, None), check_vma=False
    )
```

```python
import math

import jax
import jax.numpy as jnp
from jax import lax
from jax.experimental import pallas as pl
from jax.experimental.pallas import tpu as pltpu
from jax.sharding import Mesh
from jax.sharding import PartitionSpec as P

SAMPLES = 2048
HALF = 1024
BAND = 512
FB = 128
TB = 256
BAND_LO = 128
DEC = 8
CHANNELS = 4096
epsilon = 1e-06
bf16 = jnp.bfloat16
f32 = jnp.float32
VMEM = pl.BlockSpec(memory_space=pltpu.VMEM)
SMEM = pl.BlockSpec(memory_space=pltpu.SMEM)


def half_turn(u):
    v = u * u
    s = 1.0 + v * (-1 / 6 + v * (1 / 120 + v * (-1 / 5040 + v * (1 / 362880 + v * (-1 / 39916800)))))
    c = 1.0 + v * (
        -1 / 2 + v * (1 / 24 + v * (-1 / 720 + v * (1 / 40320 + v * (-1 / 3628800 + v * (1 / 479001600)))))
    )
    return -(u * s), c


def circle(p):
    c, s = half_turn(((p & (SAMPLES - 1)) - HALF).astype(f32) * (math.pi / SAMPLES))
    return c * c - s * s, 2.0 * c * s


def iota(dims, axis):
    return lax.broadcasted_iota(jnp.int32, dims, axis)


def delay_kernel(ids, d_ref, mine, far, cross, rows):
    xh, core = ids[0], ids[1]
    for m in range(8):
        rows[pl.ds(128 * m, 128), :] = d_ref[:, pl.ds(128 * m, 128)].astype(f32).T

    def nodes(h, b, j):
        first = (2 * (xh ^ h) + j) * 16
        parts = []
        for zy in range(16):
            at = pl.multiple_of(((first + zy) * 2 + (core ^ b)) * 8, 8)
            parts.append(rows[pl.ds(at, 8), :])
        return jnp.concatenate(parts, axis=0).T.astype(jnp.int32)

    for j in range(2):
        mine[j] = nodes(0, 0, j)
        far[j] = nodes(1, 0, j)
        for h in range(2):
            cross[h, j] = nodes(h, 1, j)


def times_kernel(offs, after, q_ref):
    scale = 1.0 / math.sqrt(FB * CHANNELS)
    for w in range(2):
        c, s = circle((1 + iota((FB, TB), 0)) * (DEC * iota((FB, TB), 1) + offs[w]))
        q_ref[w, :FB] = c * scale
        q_ref[w, FB:] = s * -scale


def table_kernel(after, fwd_ref, inv_ref, env_ref, base):
    wide = BAND + FB
    lane = iota((32, wide), 1)
    freq = jnp.where(lane < BAND, BAND_LO + lane, lane - BAND + 1)
    step = iota((32, wide), 0) * freq
    base[0], base[1] = circle(32 * step)
    cb, sb = circle(step)
    _, taper = circle(2 * iota((1, BAND), 1) + 1)
    weight = taper * taper * (2.0 / SAMPLES)

    def body(a, _):
        ca, sa = base[0, pl.ds(a, 1), :], base[1, pl.ds(a, 1), :]
        c, s = ca * cb - sa * sb, sa * cb + ca * sb
        at = pl.ds(pl.multiple_of(32 * a, 32), 32)
        fwd_ref[at, :BAND] = c[:, :BAND].astype(bf16)
        fwd_ref[at, BAND:] = (-s[:, :BAND]).astype(bf16)
        inv_ref[at, :BAND] = (weight * c[:, :BAND]).astype(bf16)
        inv_ref[at, BAND:] = (weight * s[:, :BAND]).astype(bf16)
        env_ref[at, :FB] = c[:, BAND:].astype(bf16)
        env_ref[at, FB:] = (-s[:, BAND:]).astype(bf16)
        return 0

    lax.fori_loop(0, 32, body, 0)


def front_kernel(ids, own_ref, peer_ref, fwd_ref, inv_ref, env_ref, e_ref, lhs_ref, lhs):
    tm = ids[2]
    own = own_ref[pl.ds(2 * tm, 2)].reshape(64, HALF)
    peer = peer_ref[...].reshape(64, HALF)
    terms = jnp.dot(jnp.concatenate([own, peer], axis=0), fwd_ref[...], preferred_element_type=f32)
    col = lax.broadcasted_iota(jnp.int32, (1, 2 * BAND), 1)
    sign = (1 - 2 * (col & 1)).astype(f32)
    first = jnp.where(tm == 0, jnp.ones_like(sign), sign)
    second = jnp.where(tm == 0, sign, jnp.ones_like(sign))
    spectrum = terms[:64] * first + terms[64:] * second
    both = jnp.concatenate([spectrum, spectrum * sign], axis=0)
    re, im = both[:, :BAND], both[:, BAND:]
    real_form = jnp.concatenate([re, -im], axis=1)
    imag_form = jnp.concatenate([im, re], axis=1)
    forms = jnp.concatenate([real_form, imag_form], axis=0).astype(bf16)
    analytic = lax.dot_general(forms, inv_ref[...], (((1,), (1,)), ((), ())), preferred_element_type=f32)
    real, imag = analytic[:128], analytic[128:]
    energy = real * real + imag * imag
    sums = jnp.sum(energy, axis=1, keepdims=True)
    sums = sums[:64] + sums[64:]
    env = jnp.dot(energy.astype(bf16), env_ref[...], preferred_element_type=f32)
    lane = lax.broadcasted_iota(jnp.int32, (1, 2 * FB), 1)
    odd = (2 * (lane & 1) - 1).astype(f32)
    env = env[:64] + env[64:] * odd
    factor = 1.0 / (math.sqrt(SAMPLES) * (sums / SAMPLES + epsilon))
    normal = (env * factor).astype(bf16)
    e_ref[...] = normal
    expand(normal, lhs)
    lhs_ref[...] = lhs[...].astype(bf16)


def expand(normal, lhs):
    normal = normal.astype(f32)
    kept = (iota((FB, 128), 0) & 1) == (iota((FB, 128), 1) >> 6)
    for w in range(2):
        re = normal[32 * w : 32 * w + 32, :FB]
        im = normal[32 * w : 32 * w + 32, FB:]
        for part, quad in enumerate(((re, -im, re, -im), (im, re, im, re))):
            t = jnp.concatenate(quad, axis=0).T
            lhs[pl.ds(2 * w + part, FB, stride=4), :] = jnp.where(kept, t, 0.0)


def turn(u, v):
    return u[0] * v[0] - u[1] * v[1], u[0] * v[1] + u[1] * v[0]


def stack(delays, lhs, store):
    one = [half_turn((d - 512).astype(f32) * (math.pi / 1024)) for d in delays]
    two = [turn(v, v) for v in one]
    mid = two
    for i in range(FB // 4):
        powers, ahead = [[], [], [], []], []
        for (c, s), (c1, s1), v2 in zip(mid, one, two):
            cc, ss, cs, sc = c * c1, s * s1, c * s1, s * c1
            last = turn((c, s), v2)
            for group, v in zip(powers, ((cc + ss, sc - cs), (c, s), (cc - ss, sc + cs), last)):
                group.append([x.astype(bf16) for x in v])
            ahead.append(turn(last, v2))
        mid = ahead
        at = 16 * i
        a = jnp.concatenate([v[at : at + 16, :] for v in lhs], axis=1)
        for g in range(2):
            z = [x for even, odd in zip(powers[2 * g], powers[2 * g + 1]) for x in (*even, *odd)]
            r = jnp.dot(a, jnp.concatenate(z, axis=0), preferred_element_type=f32)
            store(at + 8 * g, r[8 * g : 8 * g + 8])


def near_kernel(own_d, core_d, own_lhs, core_lhs, acc_ref):
    for j in range(2):

        def store(at, r):
            acc_ref[j, at : at + 8, :] = r

        stack((own_d[j], core_d[0, j]), (own_lhs, core_lhs), store)


def far_kernel(far_d, far_e, diag_e, acc_ref, out_ref, wide, lhs, acc):
    for i, e in enumerate((far_e, diag_e)):
        expand(e[...], wide)
        lhs[i] = wide[...].astype(bf16)
    for j in range(2):

        def store(at, r):
            acc[at : at + 8, :] = acc_ref[j, at : at + 8, :] + r

        stack((far_d[0, j], far_d[1, j]), (lhs.at[0], lhs.at[1]), store)
        for q in range(4):
            out_ref[128 * j : 128 * j + 128, 128 * q : 128 * q + 128] = acc[pl.ds(q, FB, stride=4), :].T.astype(bf16)


def final_kernel(part_ref, q_ref, out_ref):
    total = part_ref[0:16, :].astype(f32)
    for i in range(1, 16):
        total = total + part_ref[16 * i : 16 * i + 16, :].astype(f32)
    total = total[:8] + total[8:]
    for w in range(2):
        out_ref[w] = jnp.dot(
            total[:, w * TB : (w + 1) * TB], q_ref[w], precision=lax.Precision.HIGHEST, preferred_element_type=f32
        )


def call(kernel, outs, ins, scratch=(), limit=24):
    return pl.pallas_call(
        kernel,
        out_shape=outs,
        in_specs=ins,
        out_specs=jax.tree.map(lambda _: VMEM, outs),
        scratch_shapes=list(scratch),
        compiler_params=pltpu.CompilerParams(vmem_limit_bytes=limit << 20),
    )


def flip(v, *axes):
    n = 2 ** len(axes)
    return lax.ppermute(v, axes, [(i, n - 1 - i) for i in range(n)])


def shape(dims, dtype):
    return jax.ShapeDtypeStruct(dims, dtype)


def on_device(traces, delays, offsets):
    tm = lax.axis_index("tm")
    ids = jnp.stack([lax.axis_index(a) for a in ("xh", "core", "tm")]).astype(jnp.int32)
    rows = traces.transpose(1, 0, 2)
    send = jnp.where(tm == 0, rows[2:], rows[:2])
    send, ids = lax.optimization_barrier((send, ids))
    peer = flip(send, "tm")
    pair = shape((2, 32, 128), jnp.int32)
    mine, far, cross = call(
        delay_kernel, (pair, pair, shape((2, 2, 32, 128), jnp.int32)), [SMEM, VMEM], [pltpu.VMEM((1024, 32), f32)]
    )(ids, delays.T)
    crossed = flip(cross, "core")
    fwd, inv, env = call(
        table_kernel,
        (shape((HALF, 2 * BAND), bf16), shape((HALF, 2 * BAND), bf16), shape((HALF, 2 * FB), bf16)),
        [VMEM],
        [pltpu.VMEM((2, 32, BAND + FB), f32)],
    )(mine)
    peer, crossed, fwd = lax.optimization_barrier((peer, crossed, fwd))
    far_d = flip(jnp.stack([far, crossed[1]]), "xh")
    e, lhs = call(
        front_kernel,
        (shape((64, 2 * FB), bf16), shape((512, 128), bf16)),
        [SMEM] + [VMEM] * 5,
        [pltpu.VMEM((512, 128), f32)],
    )(ids, rows, peer, fwd, inv, env)
    core_lhs = flip(lhs, "core")
    far_e = flip(e, "xh")
    diag_e = flip(e, "xh", "core")
    acc = call(near_kernel, shape((2, 512, 128), f32), [VMEM] * 4)(mine, crossed, lhs, core_lhs)
    offsets, e = lax.optimization_barrier((offsets, e))
    q = call(times_kernel, shape((2, 2 * FB, TB), f32), [SMEM, VMEM])(offsets, e)
    part = call(
        far_kernel,
        shape((256, 512), bf16),
        [VMEM] * 4,
        [pltpu.VMEM((512, 128), f32), pltpu.VMEM((2, 512, 128), bf16), pltpu.VMEM((512, 128), f32)],
    )(far_d, far_e, diag_e, acc)
    parts = lax.all_to_all(part.reshape(32, 8, 512), ("xl", "zh", "y"), 0, 0, tiled=True)
    return call(final_kernel, shape((2, 8, TB), f32), [VMEM] * 2)(parts.reshape(256, 512), q)


def solution(mesh):
    chan = ("xh", "xl", "zh", "y", "core")
    fine = Mesh(mesh.devices.reshape(2, 2, 4, 4, 2, 2), chan + ("tm",))
    placed = (P(chan, None, "tm"), P(None, chan), P("tm"))
    return jax.shard_map(
        on_device, mesh=fine, in_specs=placed, out_specs=P("tm", chan, None), check_vma=False
    )
```

```python
import math

import jax
import jax.numpy as jnp
from jax import lax
from jax.experimental import pallas as pl
from jax.experimental.pallas import tpu as pltpu
from jax.sharding import Mesh
from jax.sharding import PartitionSpec as P

SAMPLES = 2048
HALF = 1024
BAND = 512
FB = 128
TB = 256
BAND_LO = 128
DEC = 8
CHANNELS = 4096
epsilon = 1e-06
bf16 = jnp.bfloat16
f32 = jnp.float32
VMEM = pl.BlockSpec(memory_space=pltpu.VMEM)
SMEM = pl.BlockSpec(memory_space=pltpu.SMEM)


def half_turn(u):
    v = u * u
    s = 1.0 + v * (-1 / 6 + v * (1 / 120 + v * (-1 / 5040 + v * (1 / 362880 + v * (-1 / 39916800)))))
    c = 1.0 + v * (
        -1 / 2 + v * (1 / 24 + v * (-1 / 720 + v * (1 / 40320 + v * (-1 / 3628800 + v * (1 / 479001600)))))
    )
    return -(u * s), c


def circle(p):
    c, s = half_turn(((p & (SAMPLES - 1)) - HALF).astype(f32) * (math.pi / SAMPLES))
    return c * c - s * s, 2.0 * c * s


def iota(dims, axis):
    return lax.broadcasted_iota(jnp.int32, dims, axis)


def delay_kernel(ids, d_ref, mine, far, cross, rows):
    xh, core = ids[0], ids[1]
    for m in range(8):
        rows[pl.ds(128 * m, 128), :] = d_ref[:, pl.ds(128 * m, 128)].astype(f32).T

    def nodes(h, b, j):
        first = (2 * (xh ^ h) + j) * 16
        parts = []
        for zy in range(16):
            at = pl.multiple_of(((first + zy) * 2 + (core ^ b)) * 8, 8)
            parts.append(rows[pl.ds(at, 8), :])
        return jnp.concatenate(parts, axis=0).T.astype(jnp.int32)

    for j in range(2):
        mine[j] = nodes(0, 0, j)
        far[j] = nodes(1, 0, j)
        for h in range(2):
            cross[h, j] = nodes(h, 1, j)


def split(v):
    high = v.astype(bf16).astype(f32)
    middle = (v - high).astype(bf16).astype(f32)
    return high, middle, (v - high) - middle


def times_kernel(offs, after, q_ref):
    scale = 1.0 / math.sqrt(FB * CHANNELS)
    for w in range(2):
        c, s = circle((1 + iota((FB, TB), 0)) * (DEC * iota((FB, TB), 1) + offs[w]))
        for i, (re, im) in enumerate(zip(split(c * scale), split(s * -scale))):
            q_ref[w, i, :FB] = re.astype(bf16)
            q_ref[w, i, FB:] = im.astype(bf16)


def table_kernel(after, fwd_ref, inv_ref, env_ref, base):
    wide = BAND + FB
    lane = iota((32, wide), 1)
    freq = jnp.where(lane < BAND, BAND_LO + lane, lane - BAND + 1)
    step = iota((32, wide), 0) * freq
    base[0], base[1] = circle(32 * step)
    cb, sb = circle(step)
    _, taper = circle(2 * iota((1, BAND), 1) + 1)
    weight = taper * taper * (2.0 / SAMPLES)

    def body(a, _):
        ca, sa = base[0, pl.ds(a, 1), :], base[1, pl.ds(a, 1), :]
        c, s = ca * cb - sa * sb, sa * cb + ca * sb
        at = pl.ds(pl.multiple_of(32 * a, 32), 32)
        fwd_ref[at, :BAND] = c[:, :BAND].astype(bf16)
        fwd_ref[at, BAND:] = (-s[:, :BAND]).astype(bf16)
        inv_ref[at, :BAND] = (weight * c[:, :BAND]).astype(bf16)
        inv_ref[at, BAND:] = (weight * s[:, :BAND]).astype(bf16)
        env_ref[at, :FB] = c[:, BAND:].astype(bf16)
        env_ref[at, FB:] = (-s[:, BAND:]).astype(bf16)
        return 0

    lax.fori_loop(0, 32, body, 0)


def front_kernel(ids, own_ref, peer_ref, fwd_ref, inv_ref, env_ref, e_ref, lhs_ref, lhs):
    tm = ids[2]
    own = own_ref[pl.ds(2 * tm, 2)].reshape(64, HALF)
    peer = peer_ref[...].reshape(64, HALF)
    terms = jnp.dot(jnp.concatenate([own, peer], axis=0), fwd_ref[...], preferred_element_type=f32)
    col = lax.broadcasted_iota(jnp.int32, (1, 2 * BAND), 1)
    sign = (1 - 2 * (col & 1)).astype(f32)
    first = jnp.where(tm == 0, jnp.ones_like(sign), sign)
    second = jnp.where(tm == 0, sign, jnp.ones_like(sign))
    spectrum = terms[:64] * first + terms[64:] * second
    both = jnp.concatenate([spectrum, spectrum * sign], axis=0)
    re, im = both[:, :BAND], both[:, BAND:]
    real_form = jnp.concatenate([re, -im], axis=1)
    imag_form = jnp.concatenate([im, re], axis=1)
    forms = jnp.concatenate([real_form, imag_form], axis=0).astype(bf16)
    analytic = lax.dot_general(forms, inv_ref[...], (((1,), (1,)), ((), ())), preferred_element_type=f32)
    real, imag = analytic[:128], analytic[128:]
    energy = real * real + imag * imag
    sums = jnp.sum(energy, axis=1, keepdims=True)
    sums = sums[:64] + sums[64:]
    env = jnp.dot(energy.astype(bf16), env_ref[...], preferred_element_type=f32)
    lane = lax.broadcasted_iota(jnp.int32, (1, 2 * FB), 1)
    odd = (2 * (lane & 1) - 1).astype(f32)
    env = env[:64] + env[64:] * odd
    factor = 1.0 / (math.sqrt(SAMPLES) * (sums / SAMPLES + epsilon))
    normal = (env * factor).astype(bf16)
    e_ref[...] = normal
    expand(normal, lhs)
    lhs_ref[...] = lhs[...].astype(bf16)


def expand(normal, lhs):
    normal = normal.astype(f32)
    kept = (iota((FB, 128), 0) & 1) == (iota((FB, 128), 1) >> 6)
    for w in range(2):
        re = normal[32 * w : 32 * w + 32, :FB]
        im = normal[32 * w : 32 * w + 32, FB:]
        for part, quad in enumerate(((re, -im, re, -im), (im, re, im, re))):
            t = jnp.concatenate(quad, axis=0).T
            lhs[pl.ds(2 * w + part, FB, stride=4), :] = jnp.where(kept, t, 0.0)


def turn(u, v):
    return u[0] * v[0] - u[1] * v[1], u[0] * v[1] + u[1] * v[0]


def stack(delays, lhs, store):
    one = [half_turn((d - 512).astype(f32) * (math.pi / 1024)) for d in delays]
    two = [turn(v, v) for v in one]
    mid = two
    for i in range(FB // 4):
        powers, ahead = [[], [], [], []], []
        for (c, s), (c1, s1), v2 in zip(mid, one, two):
            cc, ss, cs, sc = c * c1, s * s1, c * s1, s * c1
            last = turn((c, s), v2)
            for group, v in zip(powers, ((cc + ss, sc - cs), (c, s), (cc - ss, sc + cs), last)):
                group.append([x.astype(bf16) for x in v])
            ahead.append(turn(last, v2))
        mid = ahead
        at = 16 * i
        a = jnp.concatenate([v[at : at + 16, :] for v in lhs], axis=1)
        for g in range(2):
            z = [x for even, odd in zip(powers[2 * g], powers[2 * g + 1]) for x in (*even, *odd)]
            r = jnp.dot(a, jnp.concatenate(z, axis=0), preferred_element_type=f32)
            store(at + 8 * g, r[8 * g : 8 * g + 8])


def near_kernel(own_d, core_d, own_lhs, core_e, acc_ref, wide, core_lhs):
    expand(core_e[...], wide)
    core_lhs[...] = wide[...].astype(bf16)
    for j in range(2):

        def store(at, r):
            acc_ref[j, at : at + 8, :] = r

        stack((own_d[j], core_d[0, j]), (own_lhs, core_lhs), store)


def far_kernel(far_d, far_e, acc_ref, out_ref, wide, lhs, acc):
    for i in range(2):
        expand(far_e[i], wide)
        lhs[i] = wide[...].astype(bf16)
    for j in range(2):

        def store(at, r):
            acc[at : at + 8, :] = acc_ref[j, at : at + 8, :] + r

        stack((far_d[0, j], far_d[1, j]), (lhs.at[0], lhs.at[1]), store)
        for q in range(4):
            out_ref[128 * j : 128 * j + 128, 128 * q : 128 * q + 128] = acc[pl.ds(q, FB, stride=4), :].T.astype(bf16)


def final_kernel(part_ref, q_ref, out_ref):
    total = part_ref[0:16, :].astype(f32)
    for i in range(1, 16):
        total = total + part_ref[16 * i : 16 * i + 16, :].astype(f32)
    total = total[:8] + total[8:]
    zero = jnp.zeros((8, TB), f32)
    for w in range(2):
        a = jnp.concatenate([*split(total[:, w * TB : (w + 1) * TB]), zero], axis=0).astype(bf16)
        r = [jnp.dot(a, q_ref[w, i], preferred_element_type=f32) for i in range(3)]
        out_ref[w] = (r[0][:8] + ((r[0][8:16] + r[1][:8]) + ((r[0][16:24] + r[1][8:16]) + r[2][:8])))


def call(kernel, outs, ins, scratch=(), limit=24):
    return pl.pallas_call(
        kernel,
        out_shape=outs,
        in_specs=ins,
        out_specs=jax.tree.map(lambda _: VMEM, outs),
        scratch_shapes=list(scratch),
        compiler_params=pltpu.CompilerParams(vmem_limit_bytes=limit << 20),
    )


def flip(v, *axes):
    n = 2 ** len(axes)
    return lax.ppermute(v, axes, [(i, n - 1 - i) for i in range(n)])


def shape(dims, dtype):
    return jax.ShapeDtypeStruct(dims, dtype)


def on_device(traces, delays, offsets):
    tm = lax.axis_index("tm")
    ids = jnp.stack([lax.axis_index(a) for a in ("xh", "core", "tm")]).astype(jnp.int32)
    rows = traces.transpose(1, 0, 2)
    send = jnp.where(tm == 0, rows[2:], rows[:2])
    send, ids = lax.optimization_barrier((send, ids))
    peer = flip(send, "tm")
    pair = shape((2, 32, 128), jnp.int32)
    mine, far, cross = call(
        delay_kernel, (pair, pair, shape((2, 2, 32, 128), jnp.int32)), [SMEM, VMEM], [pltpu.VMEM((1024, 32), f32)]
    )(ids, delays.T)
    core_d = flip(cross, "core")
    fwd, inv, env = call(
        table_kernel,
        (shape((HALF, 2 * BAND), bf16), shape((HALF, 2 * BAND), bf16), shape((HALF, 2 * FB), bf16)),
        [VMEM],
        [pltpu.VMEM((2, 32, BAND + FB), f32)],
    )(mine)
    peer, core_d, fwd = lax.optimization_barrier((peer, core_d, fwd))
    e, lhs = call(
        front_kernel,
        (shape((64, 2 * FB), bf16), shape((512, 128), bf16)),
        [SMEM] + [VMEM] * 5,
        [pltpu.VMEM((512, 128), f32)],
    )(ids, rows, peer, fwd, inv, env)
    far_d = flip(jnp.stack([far, core_d[1]]), "xh")
    core_e = flip(e, "core")
    far_e = flip(jnp.stack([e, core_e]), "xh")
    acc = call(
        near_kernel,
        shape((2, 512, 128), f32),
        [VMEM] * 4,
        [pltpu.VMEM((512, 128), f32), pltpu.VMEM((512, 128), bf16)],
    )(mine, core_d, lhs, core_e)
    offsets, e = lax.optimization_barrier((offsets, acc[0, :8]))
    q = call(times_kernel, shape((2, 3, 2 * FB, TB), bf16), [SMEM, VMEM])(offsets, e)
    q, acc = lax.optimization_barrier((q, acc))
    part = call(
        far_kernel,
        shape((256, 512), bf16),
        [VMEM] * 3,
        [pltpu.VMEM((512, 128), f32), pltpu.VMEM((2, 512, 128), bf16), pltpu.VMEM((512, 128), f32)],
    )(far_d, far_e, acc)
    parts = lax.all_to_all(part.reshape(32, 8, 512), ("xl", "zh", "y"), 0, 0, tiled=True)
    return call(final_kernel, shape((2, 8, TB), f32), [VMEM] * 2)(parts.reshape(256, 512), q)


def solution(mesh):
    chan = ("xh", "xl", "zh", "y", "core")
    fine = Mesh(mesh.devices.reshape(2, 2, 4, 4, 2, 2), chan + ("tm",))
    placed = (P(chan, None, "tm"), P(None, chan), P("tm"))
    return jax.shard_map(
        on_device, mesh=fine, in_specs=placed, out_specs=P("tm", chan, None), check_vma=False
    )
```

```python
import math

import jax
import jax.numpy as jnp
from jax import lax
from jax.experimental import pallas as pl
from jax.experimental.pallas import tpu as pltpu
from jax.sharding import Mesh
from jax.sharding import PartitionSpec as P

SAMPLES = 2048
HALF = 1024
BAND = 512
FB = 128
TB = 256
BAND_LO = 128
DEC = 8
CHANNELS = 4096
epsilon = 1e-06
bf16 = jnp.bfloat16
f32 = jnp.float32
VMEM = pl.BlockSpec(memory_space=pltpu.VMEM)
SMEM = pl.BlockSpec(memory_space=pltpu.SMEM)


def half_turn(u):
    v = u * u
    s = 1.0 + v * (-1 / 6 + v * (1 / 120 + v * (-1 / 5040 + v * (1 / 362880 + v * (-1 / 39916800)))))
    c = 1.0 + v * (
        -1 / 2 + v * (1 / 24 + v * (-1 / 720 + v * (1 / 40320 + v * (-1 / 3628800 + v * (1 / 479001600)))))
    )
    return -(u * s), c


def circle(p):
    c, s = half_turn(((p & (SAMPLES - 1)) - HALF).astype(f32) * (math.pi / SAMPLES))
    return c * c - s * s, 2.0 * c * s


def iota(dims, axis):
    return lax.broadcasted_iota(jnp.int32, dims, axis)


def delay_kernel(ids, d_ref, mine, far, cross, rows):
    xl, core = ids[0], ids[1]
    for m in range(8):
        rows[pl.ds(128 * m, 128), :] = d_ref[:, pl.ds(128 * m, 128)].astype(f32).T

    def nodes(h, b, j):
        first = (2 * j + (xl ^ h)) * 16
        parts = []
        for zy in range(16):
            at = pl.multiple_of(((first + zy) * 2 + (core ^ b)) * 8, 8)
            parts.append(rows[pl.ds(at, 8), :])
        return jnp.concatenate(parts, axis=0).T.astype(jnp.int32)

    for j in range(2):
        mine[j] = nodes(0, 0, j)
        far[j] = nodes(1, 0, j)
        for h in range(2):
            cross[h, j] = nodes(h, 1, j)


def split(v):
    high = v.astype(bf16).astype(f32)
    middle = (v - high).astype(bf16).astype(f32)
    return high, middle, (v - high) - middle


def times_kernel(offs, after, q_ref):
    scale = 1.0 / math.sqrt(FB * CHANNELS)
    for w in range(2):
        c, s = circle((1 + iota((FB, TB), 0)) * (DEC * iota((FB, TB), 1) + offs[w]))
        for i, (re, im) in enumerate(zip(split(c * scale), split(s * -scale))):
            q_ref[w, i, :FB] = re.astype(bf16)
            q_ref[w, i, FB:] = im.astype(bf16)


def table_kernel(after, fwd_ref, inv_ref, env_ref, base):
    wide = BAND + FB
    lane = iota((32, wide), 1)
    freq = jnp.where(lane < BAND, BAND_LO + lane, lane - BAND + 1)
    step = iota((32, wide), 0) * freq
    base[0], base[1] = circle(32 * step)
    cb, sb = circle(step)
    _, taper = circle(2 * iota((1, BAND), 1) + 1)
    weight = taper * taper * (2.0 / SAMPLES)

    def body(a, _):
        ca, sa = base[0, pl.ds(a, 1), :], base[1, pl.ds(a, 1), :]
        c, s = ca * cb - sa * sb, sa * cb + ca * sb
        at = pl.ds(pl.multiple_of(32 * a, 32), 32)
        fwd_ref[at, :BAND] = c[:, :BAND].astype(bf16)
        fwd_ref[at, BAND:] = (-s[:, :BAND]).astype(bf16)
        inv_ref[at, :BAND] = (weight * c[:, :BAND]).astype(bf16)
        inv_ref[at, BAND:] = (weight * s[:, :BAND]).astype(bf16)
        env_ref[at, :FB] = c[:, BAND:].astype(bf16)
        env_ref[at, FB:] = (-s[:, BAND:]).astype(bf16)
        return 0

    lax.fori_loop(0, 32, body, 0)


def front_kernel(ids, own_ref, peer_ref, fwd_ref, inv_ref, env_ref, e_ref):
    tm = ids[2]
    own = own_ref[pl.ds(2 * tm, 2)].reshape(64, HALF)
    peer = peer_ref[...].reshape(64, HALF)
    terms = jnp.dot(jnp.concatenate([own, peer], axis=0), fwd_ref[...], preferred_element_type=f32)
    col = lax.broadcasted_iota(jnp.int32, (1, 2 * BAND), 1)
    sign = (1 - 2 * (col & 1)).astype(f32)
    first = jnp.where(tm == 0, jnp.ones_like(sign), sign)
    second = jnp.where(tm == 0, sign, jnp.ones_like(sign))
    spectrum = terms[:64] * first + terms[64:] * second
    both = jnp.concatenate([spectrum, spectrum * sign], axis=0)
    re, im = both[:, :BAND], both[:, BAND:]
    real_form = jnp.concatenate([re, -im], axis=1)
    imag_form = jnp.concatenate([im, re], axis=1)
    forms = jnp.concatenate([real_form, imag_form], axis=0).astype(bf16)
    analytic = lax.dot_general(forms, inv_ref[...], (((1,), (1,)), ((), ())), preferred_element_type=f32)
    real, imag = analytic[:128], analytic[128:]
    energy = real * real + imag * imag
    sums = jnp.sum(energy, axis=1, keepdims=True)
    sums = sums[:64] + sums[64:]
    env = jnp.dot(energy.astype(bf16), env_ref[...], preferred_element_type=f32)
    lane = lax.broadcasted_iota(jnp.int32, (1, 2 * FB), 1)
    odd = (2 * (lane & 1) - 1).astype(f32)
    env = env[:64] + env[64:] * odd
    factor = 1.0 / (math.sqrt(SAMPLES) * (sums / SAMPLES + epsilon))
    e_ref[...] = (env * factor).astype(bf16)


def expand(normal, lhs):
    normal = normal.astype(f32)
    kept = (iota((FB, 128), 0) & 1) == (iota((FB, 128), 1) >> 6)
    for w in range(2):
        re = normal[32 * w : 32 * w + 32, :FB]
        im = normal[32 * w : 32 * w + 32, FB:]
        for part, quad in enumerate(((re, -im, re, -im), (im, re, im, re))):
            t = jnp.concatenate(quad, axis=0).T
            lhs[pl.ds(2 * w + part, FB, stride=4), :] = jnp.where(kept, t, 0.0)


def turn(u, v):
    return u[0] * v[0] - u[1] * v[1], u[0] * v[1] + u[1] * v[0]


def stack(delays, lhs, store):
    one = [half_turn((d - 512).astype(f32) * (math.pi / 1024)) for d in delays]
    two = [turn(v, v) for v in one]
    mid = two
    for i in range(FB // 4):
        powers, ahead = [[], [], [], []], []
        for (c, s), (c1, s1), v2 in zip(mid, one, two):
            cc, ss, cs, sc = c * c1, s * s1, c * s1, s * c1
            last = turn((c, s), v2)
            for group, v in zip(powers, ((cc + ss, sc - cs), (c, s), (cc - ss, sc + cs), last)):
                group.append([x.astype(bf16) for x in v])
            ahead.append(turn(last, v2))
        mid = ahead
        at = 16 * i
        a = jnp.concatenate([v[at : at + 16, :] for v in lhs], axis=1)
        for g in range(2):
            z = [x for even, odd in zip(powers[2 * g], powers[2 * g + 1]) for x in (*even, *odd)]
            r = jnp.dot(a, jnp.concatenate(z, axis=0), preferred_element_type=f32)
            store(at + 8 * g, r[8 * g : 8 * g + 8])


def near_kernel(own_d, core_d, own_e, core_e, acc_ref, wide, lhs):
    for i, e in enumerate((own_e, core_e)):
        expand(e[...], wide)
        lhs[i] = wide[...].astype(bf16)
    for j in range(2):

        def store(at, r):
            acc_ref[j, at : at + 8, :] = r

        stack((own_d[j], core_d[0, j]), (lhs.at[0], lhs.at[1]), store)


def far_kernel(far_d, far_e, acc_ref, out_ref, wide, lhs, acc):
    for i in range(2):
        expand(far_e[i], wide)
        lhs[i] = wide[...].astype(bf16)
    for j in range(2):

        def store(at, r):
            acc[at : at + 8, :] = acc_ref[j, at : at + 8, :] + r

        stack((far_d[0, j], far_d[1, j]), (lhs.at[0], lhs.at[1]), store)
        for q in range(4):
            out_ref[128 * j : 128 * j + 128, 128 * q : 128 * q + 128] = acc[pl.ds(q, FB, stride=4), :].T.astype(bf16)


def final_kernel(part_ref, q_ref, out_ref):
    total = part_ref[0:16, :].astype(f32)
    for i in range(1, 16):
        total = total + part_ref[16 * i : 16 * i + 16, :].astype(f32)
    total = total[:8] + total[8:]
    zero = jnp.zeros((8, TB), f32)
    for w in range(2):
        a = jnp.concatenate([*split(total[:, w * TB : (w + 1) * TB]), zero], axis=0).astype(bf16)
        r = [jnp.dot(a, q_ref[w, i], preferred_element_type=f32) for i in range(3)]
        out_ref[w] = (r[0][:8] + ((r[0][8:16] + r[1][:8]) + ((r[0][16:24] + r[1][8:16]) + r[2][:8])))


def call(kernel, outs, ins, scratch=(), limit=24):
    return pl.pallas_call(
        kernel,
        out_shape=outs,
        in_specs=ins,
        out_specs=jax.tree.map(lambda _: VMEM, outs),
        scratch_shapes=list(scratch),
        compiler_params=pltpu.CompilerParams(vmem_limit_bytes=limit << 20),
    )


def flip(v, *axes):
    n = 2 ** len(axes)
    return lax.ppermute(v, axes, [(i, n - 1 - i) for i in range(n)])


def shape(dims, dtype):
    return jax.ShapeDtypeStruct(dims, dtype)


def on_device(traces, delays, offsets):
    tm = lax.axis_index("tm")
    ids = jnp.stack([lax.axis_index(a) for a in ("xl", "core", "tm")]).astype(jnp.int32)
    rows = traces.transpose(1, 0, 2)
    send = jnp.where(tm == 0, rows[2:], rows[:2])
    send, ids = lax.optimization_barrier((send, ids))
    peer = flip(send, "tm")
    pair = shape((2, 32, 128), jnp.int32)
    mine, far, cross = call(
        delay_kernel, (pair, pair, shape((2, 2, 32, 128), jnp.int32)), [SMEM, VMEM], [pltpu.VMEM((1024, 32), f32)]
    )(ids, delays.T)
    core_d = flip(cross, "core")
    fwd, inv, env = call(
        table_kernel,
        (shape((HALF, 2 * BAND), bf16), shape((HALF, 2 * BAND), bf16), shape((HALF, 2 * FB), bf16)),
        [VMEM],
        [pltpu.VMEM((2, 32, BAND + FB), f32)],
    )(mine)
    peer, core_d, fwd = lax.optimization_barrier((peer, core_d, fwd))
    e = call(front_kernel, shape((64, 2 * FB), bf16), [SMEM] + [VMEM] * 5)(ids, rows, peer, fwd, inv, env)
    far_d = flip(jnp.stack([far, core_d[1]]), "xl")
    core_e = flip(e, "core")
    far_e = flip(jnp.stack([e, core_e]), "xl")
    acc = call(
        near_kernel,
        shape((2, 512, 128), f32),
        [VMEM] * 4,
        [pltpu.VMEM((512, 128), f32), pltpu.VMEM((2, 512, 128), bf16)],
    )(mine, core_d, e, core_e)
    offsets, after = lax.optimization_barrier((offsets, acc[0, :8]))
    q = call(times_kernel, shape((2, 3, 2 * FB, TB), bf16), [SMEM, VMEM])(offsets, after)
    q, acc = lax.optimization_barrier((q, acc))
    part = call(
        far_kernel,
        shape((256, 512), bf16),
        [VMEM] * 3,
        [pltpu.VMEM((512, 128), f32), pltpu.VMEM((2, 512, 128), bf16), pltpu.VMEM((512, 128), f32)],
    )(far_d, far_e, acc)
    parts = lax.all_to_all(part.reshape(32, 8, 512), ("xh", "zh", "y"), 0, 0, tiled=True)
    return call(final_kernel, shape((2, 8, TB), f32), [VMEM] * 2)(parts.reshape(256, 512), q)


def solution(mesh):
    chan = ("xh", "xl", "zh", "y", "core")
    fine = Mesh(mesh.devices.reshape(2, 2, 4, 4, 2, 2), chan + ("tm",))
    placed = (P(chan, None, "tm"), P(None, chan), P("tm"))
    return jax.shard_map(
        on_device, mesh=fine, in_specs=placed, out_specs=P("tm", chan, None), check_vma=False
    )
```

```python
import math

import jax
import jax.numpy as jnp
from jax import lax
from jax.experimental import pallas as pl
from jax.experimental.pallas import tpu as pltpu
from jax.sharding import Mesh
from jax.sharding import PartitionSpec as P

SAMPLES = 2048
HALF = 1024
BAND = 512
FB = 128
TB = 256
BAND_LO = 128
DEC = 8
CHANNELS = 4096
epsilon = 1e-06
bf16 = jnp.bfloat16
f32 = jnp.float32
VMEM = pl.BlockSpec(memory_space=pltpu.VMEM)
SMEM = pl.BlockSpec(memory_space=pltpu.SMEM)


def half_turn(u):
    v = u * u
    s = 1.0 + v * (-1 / 6 + v * (1 / 120 + v * (-1 / 5040 + v * (1 / 362880 + v * (-1 / 39916800)))))
    c = 1.0 + v * (
        -1 / 2 + v * (1 / 24 + v * (-1 / 720 + v * (1 / 40320 + v * (-1 / 3628800 + v * (1 / 479001600)))))
    )
    return -(u * s), c


def circle(p):
    c, s = half_turn(((p & (SAMPLES - 1)) - HALF).astype(f32) * (math.pi / SAMPLES))
    return c * c - s * s, 2.0 * c * s


def iota(dims, axis):
    return lax.broadcasted_iota(jnp.int32, dims, axis)


def delay_kernel(ids, d_ref, mine, cross, far, rows):
    xh, core = ids[0], ids[1]
    for m in range(8):
        rows[pl.ds(128 * m, 128), :] = d_ref[:, pl.ds(128 * m, 128)].astype(f32).T

    def nodes(h, b, j):
        first = (2 * (xh ^ h) + j) * 16
        parts = []
        for zy in range(16):
            at = pl.multiple_of(((first + zy) * 2 + (core ^ b)) * 8, 8)
            parts.append(rows[pl.ds(at, 8), :])
        return jnp.concatenate(parts, axis=0).T

    for j in range(2):
        mine[j] = nodes(0, 0, j)
        cross[j] = nodes(0, 1, j)
        for b in range(2):
            d = nodes(1, b, j).astype(jnp.int32)
            lanes = pl.ds(128 * j, 128)
            far[pl.ds(64 * b, 32), lanes] = (d >> 3).astype(f32).astype(bf16)
            far[pl.ds(64 * b + 32, 32), lanes] = (d & 7).astype(f32).astype(bf16)


def joined(ref, at, j):
    lanes = slice(128 * j, 128 * j + 128)
    return ref[at : at + 32, lanes].astype(f32) * 8.0 + ref[at + 32 : at + 64, lanes].astype(f32)


def split(v):
    high = v.astype(bf16).astype(f32)
    middle = (v - high).astype(bf16).astype(f32)
    return high, middle, (v - high) - middle


def times_kernel(offs, after, q_ref):
    scale = 1.0 / math.sqrt(FB * CHANNELS)
    for w in range(2):
        c, s = circle((1 + iota((FB, TB), 0)) * (DEC * iota((FB, TB), 1) + offs[w]))
        for i, (re, im) in enumerate(zip(split(c * scale), split(s * -scale))):
            q_ref[w, i, :FB] = re.astype(bf16)
            q_ref[w, i, FB:] = im.astype(bf16)


def table_kernel(after, fwd_ref, inv_ref, env_ref, base):
    wide = BAND + FB
    lane = iota((32, wide), 1)
    freq = jnp.where(lane < BAND, BAND_LO + lane, lane - BAND + 1)
    step = iota((32, wide), 0) * freq
    base[0], base[1] = circle(32 * step)
    cb, sb = circle(step)
    _, taper = circle(2 * iota((1, BAND), 1) + 1)
    weight = taper * taper * (2.0 / SAMPLES)

    def body(a, _):
        ca, sa = base[0, pl.ds(a, 1), :], base[1, pl.ds(a, 1), :]
        c, s = ca * cb - sa * sb, sa * cb + ca * sb
        at = pl.ds(pl.multiple_of(32 * a, 32), 32)
        fwd_ref[at, :BAND] = c[:, :BAND].astype(bf16)
        fwd_ref[at, BAND:] = (-s[:, :BAND]).astype(bf16)
        inv_ref[at, :BAND] = (weight * c[:, :BAND]).astype(bf16)
        inv_ref[at, BAND:] = (weight * s[:, :BAND]).astype(bf16)
        env_ref[at, :FB] = c[:, BAND:].astype(bf16)
        env_ref[at, FB:] = (-s[:, BAND:]).astype(bf16)
        return 0

    lax.fori_loop(0, 32, body, 0)


def front_kernel(ids, own_ref, peer_ref, fwd_ref, inv_ref, env_ref, e_ref):
    tm = ids[2]
    own = own_ref[pl.ds(2 * tm, 2)].reshape(64, HALF)
    peer = peer_ref[...].reshape(64, HALF)
    terms = jnp.dot(jnp.concatenate([own, peer], axis=0), fwd_ref[...], preferred_element_type=f32)
    col = lax.broadcasted_iota(jnp.int32, (1, 2 * BAND), 1)
    sign = (1 - 2 * (col & 1)).astype(f32)
    first = jnp.where(tm == 0, jnp.ones_like(sign), sign)
    second = jnp.where(tm == 0, sign, jnp.ones_like(sign))
    spectrum = terms[:64] * first + terms[64:] * second
    both = jnp.concatenate([spectrum, spectrum * sign], axis=0)
    re, im = both[:, :BAND], both[:, BAND:]
    real_form = jnp.concatenate([re, -im], axis=1)
    imag_form = jnp.concatenate([im, re], axis=1)
    forms = jnp.concatenate([real_form, imag_form], axis=0).astype(bf16)
    analytic = lax.dot_general(forms, inv_ref[...], (((1,), (1,)), ((), ())), preferred_element_type=f32)
    real, imag = analytic[:128], analytic[128:]
    energy = real * real + imag * imag
    sums = jnp.sum(energy, axis=1, keepdims=True)
    sums = sums[:64] + sums[64:]
    env = jnp.dot(energy.astype(bf16), env_ref[...], preferred_element_type=f32)
    lane = lax.broadcasted_iota(jnp.int32, (1, 2 * FB), 1)
    odd = (2 * (lane & 1) - 1).astype(f32)
    env = env[:64] + env[64:] * odd
    factor = 1.0 / (math.sqrt(SAMPLES) * (sums / SAMPLES + epsilon))
    e_ref[...] = (env * factor).astype(bf16)


def expand(normal, lhs):
    normal = normal.astype(f32)
    kept = (iota((FB, 128), 0) & 1) == (iota((FB, 128), 1) >> 6)
    for w in range(2):
        re = normal[32 * w : 32 * w + 32, :FB]
        im = normal[32 * w : 32 * w + 32, FB:]
        for part, quad in enumerate(((re, -im, re, -im), (im, re, im, re))):
            t = jnp.concatenate(quad, axis=0).T
            lhs[pl.ds(2 * w + part, FB, stride=4), :] = jnp.where(kept, t, 0.0)


def turn(u, v):
    return u[0] * v[0] - u[1] * v[1], u[0] * v[1] + u[1] * v[0]


def stack(delays, lhs, store):
    one = [half_turn((d - 512.0) * (math.pi / 1024)) for d in delays]
    two = [turn(v, v) for v in one]
    mid = two
    for i in range(FB // 4):
        powers, ahead = [[], [], [], []], []
        for (c, s), (c1, s1), v2 in zip(mid, one, two):
            cc, ss, cs, sc = c * c1, s * s1, c * s1, s * c1
            last = turn((c, s), v2)
            for group, v in zip(powers, ((cc + ss, sc - cs), (c, s), (cc - ss, sc + cs), last)):
                group.append([x.astype(bf16) for x in v])
            ahead.append(turn(last, v2))
        mid = ahead
        at = 16 * i
        a = jnp.concatenate([v[at : at + 16, :] for v in lhs], axis=1)
        for g in range(2):
            z = [x for even, odd in zip(powers[2 * g], powers[2 * g + 1]) for x in (*even, *odd)]
            r = jnp.dot(a, jnp.concatenate(z, axis=0), preferred_element_type=f32)
            store(at + 8 * g, r[8 * g : 8 * g + 8])


def near_kernel(own_d, core_d, own_e, core_e, acc_ref, wide, lhs):
    for i, e in enumerate((own_e, core_e)):
        expand(e[...], wide)
        lhs[i] = wide[...].astype(bf16)
    for j in range(2):

        def store(at, r):
            acc_ref[j, at : at + 8, :] = r

        stack((own_d[j], core_d[j]), (lhs.at[0], lhs.at[1]), store)


def far_kernel(message, acc_ref, out_ref, wide, lhs):
    expand(message[64:128], wide)
    lhs[...] = wide[...].astype(bf16)
    for j in range(2):

        def store(at, r):
            out_ref[j, at : at + 8, :] = acc_ref[j, at : at + 8, :] + r

        stack((joined(message, 0, j),), (lhs,), store)


def last_kernel(message, acc_ref, out_ref, wide, lhs, acc):
    expand(message[0:64], wide)
    lhs[...] = wide[...].astype(bf16)
    for j in range(2):

        def store(at, r):
            acc[at : at + 8, :] = acc_ref[j, at : at + 8, :] + r

        stack((joined(message, 64, j),), (lhs,), store)
        for q in range(4):
            out_ref[128 * j : 128 * j + 128, 128 * q : 128 * q + 128] = acc[pl.ds(q, FB, stride=4), :].T.astype(bf16)


def final_kernel(part_ref, q_ref, out_ref):
    total = part_ref[0:16, :].astype(f32)
    for i in range(1, 16):
        total = total + part_ref[16 * i : 16 * i + 16, :].astype(f32)
    total = total[:8] + total[8:]
    zero = jnp.zeros((8, TB), f32)
    for w in range(2):
        a = jnp.concatenate([*split(total[:, w * TB : (w + 1) * TB]), zero], axis=0).astype(bf16)
        r = [jnp.dot(a, q_ref[w, i], preferred_element_type=f32) for i in range(3)]
        out_ref[w] = (r[0][:8] + ((r[0][8:16] + r[1][:8]) + ((r[0][16:24] + r[1][8:16]) + r[2][:8])))


def call(kernel, outs, ins, scratch=(), limit=24):
    return pl.pallas_call(
        kernel,
        out_shape=outs,
        in_specs=ins,
        out_specs=jax.tree.map(lambda _: VMEM, outs),
        scratch_shapes=list(scratch),
        compiler_params=pltpu.CompilerParams(vmem_limit_bytes=limit << 20),
    )


def flip(v, *axes):
    n = 2 ** len(axes)
    return lax.ppermute(v, axes, [(i, n - 1 - i) for i in range(n)])


def shape(dims, dtype):
    return jax.ShapeDtypeStruct(dims, dtype)


def on_device(traces, delays, offsets):
    tm = lax.axis_index("tm")
    ids = jnp.stack([lax.axis_index(a) for a in ("xh", "core", "tm")]).astype(jnp.int32)
    rows = traces.transpose(1, 0, 2)
    send = jnp.where(tm == 0, rows[2:], rows[:2])
    send, ids = lax.optimization_barrier((send, ids))
    peer = flip(send, "tm")
    pair = shape((2, 32, 128), f32)
    mine, cross, far = call(
        delay_kernel, (pair, pair, shape((128, 256), bf16)), [SMEM, VMEM], [pltpu.VMEM((1024, 32), f32)]
    )(ids, delays.T)
    core_d = flip(cross, "core")
    fwd, inv, env = call(
        table_kernel,
        (shape((HALF, 2 * BAND), bf16), shape((HALF, 2 * BAND), bf16), shape((HALF, 2 * FB), bf16)),
        [VMEM],
        [pltpu.VMEM((2, 32, BAND + FB), f32)],
    )(mine)
    peer, core_d, fwd = lax.optimization_barrier((peer, core_d, fwd))
    e = call(front_kernel, shape((64, 2 * FB), bf16), [SMEM] + [VMEM] * 5)(ids, rows, peer, fwd, inv, env)
    core_e = flip(e, "core")
    far_message = flip(jnp.concatenate([far[:64], e, far[64:]]), "xh")
    acc = call(
        near_kernel,
        shape((2, 512, 128), f32),
        [VMEM] * 4,
        [pltpu.VMEM((512, 128), f32), pltpu.VMEM((2, 512, 128), bf16)],
    )(mine, core_d, e, core_e)
    offsets, after = lax.optimization_barrier((offsets, acc[0, :8]))
    q = call(times_kernel, shape((2, 3, 2 * FB, TB), bf16), [SMEM, VMEM])(offsets, after)
    q, acc, far_message = lax.optimization_barrier((q, acc, far_message))
    diag_message = flip(far_message[64:], "core")
    wide, lhs = pltpu.VMEM((512, 128), f32), pltpu.VMEM((512, 128), bf16)
    acc = call(far_kernel, shape((2, 512, 128), f32), [VMEM] * 2, [wide, lhs])(far_message, acc)
    part = call(
        last_kernel, shape((256, 512), bf16), [VMEM] * 2, [wide, lhs, pltpu.VMEM((512, 128), f32)]
    )(diag_message, acc)
    parts = lax.all_to_all(part.reshape(32, 8, 512), ("xl", "zh", "y"), 0, 0, tiled=True)
    return call(final_kernel, shape((2, 8, TB), f32), [VMEM] * 2)(parts.reshape(256, 512), q)


def solution(mesh):
    chan = ("xh", "xl", "zh", "y", "core")
    fine = Mesh(mesh.devices.reshape(2, 2, 4, 4, 2, 2), chan + ("tm",))
    placed = (P(chan, None, "tm"), P(None, chan), P("tm"))
    return jax.shard_map(
        on_device, mesh=fine, in_specs=placed, out_specs=P("tm", chan, None), check_vma=False
    )
```

```python
import math

import jax
import jax.numpy as jnp
from jax import lax
from jax.experimental import pallas as pl
from jax.experimental.pallas import tpu as pltpu
from jax.sharding import Mesh
from jax.sharding import PartitionSpec as P

SAMPLES = 2048
HALF = 1024
BAND = 512
FB = 128
TB = 256
BAND_LO = 128
DEC = 8
CHANNELS = 4096
epsilon = 1e-06
bf16 = jnp.bfloat16
f32 = jnp.float32
VMEM = pl.BlockSpec(memory_space=pltpu.VMEM)
SMEM = pl.BlockSpec(memory_space=pltpu.SMEM)
HBM = pl.BlockSpec(memory_space=pltpu.HBM)


def half_turn(u):
    v = u * u
    s = 1.0 + v * (-1 / 6 + v * (1 / 120 + v * (-1 / 5040 + v * (1 / 362880 + v * (-1 / 39916800)))))
    c = 1.0 + v * (
        -1 / 2 + v * (1 / 24 + v * (-1 / 720 + v * (1 / 40320 + v * (-1 / 3628800 + v * (1 / 479001600)))))
    )
    return -(u * s), c


def circle(p):
    c, s = half_turn(((p & (SAMPLES - 1)) - HALF).astype(f32) * (math.pi / SAMPLES))
    return c * c - s * s, 2.0 * c * s


def iota(dims, axis):
    return lax.broadcasted_iota(jnp.int32, dims, axis)


def turn(u, v):
    return u[0] * v[0] - u[1] * v[1], u[0] * v[1] + u[1] * v[0]


def each_block(freq, base, store):
    step = iota(freq.shape, 0) * freq
    base[0], base[1] = circle(32 * step)
    low = circle(step)

    def body(a, _):
        at = pl.ds(pl.multiple_of(32 * a, 32), 32)
        store(at, *turn((base[0, pl.ds(a, 1), :], base[1, pl.ds(a, 1), :]), low))
        return 0

    lax.fori_loop(0, 32, body, 0, unroll=2)


def first_kernel(ids, d_hbm, mine, far, cross, fwd_ref, env_ref, d_ref, rows, base, sem):
    copy = pltpu.make_async_copy(d_hbm, d_ref, sem)
    copy.start()
    lane = iota((32, BAND + FB), 1)

    def store(at, c, s):
        fwd_ref[at, :BAND] = c[:, :BAND].astype(bf16)
        fwd_ref[at, BAND:] = (-s[:, :BAND]).astype(bf16)
        env_ref[at, :FB] = c[:, BAND:].astype(bf16)
        env_ref[at, FB:] = (-s[:, BAND:]).astype(bf16)

    each_block(jnp.where(lane < BAND, BAND_LO + lane, lane - BAND + 1), base, store)
    copy.wait()
    xh, core = ids[0], ids[1]
    for m in range(8):
        rows[pl.ds(128 * m, 128), :] = d_ref[:, pl.ds(128 * m, 128)].astype(f32).T

    def nodes(h, b, j):
        parts = []
        for zh in (2 * j, 2 * j + 1):
            for y in range(4):
                for xl in range(2):
                    x = 2 * (xh ^ h) + xl
                    at = pl.multiple_of((((x * 4 + zh) * 4 + y) * 2 + (core ^ b)) * 8, 8)
                    parts.append(rows[pl.ds(at, 8), :])
        return jnp.concatenate(parts, axis=0).T.astype(jnp.int32)

    for j in range(2):
        mine[j] = nodes(0, 0, j)
        far[j] = nodes(1, 0, j)
        for h in range(2):
            cross[h, j] = nodes(h, 1, j)


def split(v):
    high = v.astype(bf16).astype(f32)
    middle = (v - high).astype(bf16).astype(f32)
    return high, middle, (v - high) - middle


def times_kernel(offs, after, q_ref):
    scale = 1.0 / math.sqrt(FB * CHANNELS)
    for w in range(2):
        c, s = circle((1 + iota((FB, TB), 0)) * (DEC * iota((FB, TB), 1) + offs[w]))
        for i, (re, im) in enumerate(zip(split(c * scale), split(s * -scale))):
            q_ref[w, i, :FB] = re.astype(bf16)
            q_ref[w, i, FB:] = im.astype(bf16)


def inverse_kernel(after, inv_ref, base):
    _, taper = circle(2 * iota((1, BAND), 1) + 1)
    weight = taper * taper * (2.0 / SAMPLES)

    def store(at, c, s):
        inv_ref[at, :BAND] = (weight * c).astype(bf16)
        inv_ref[at, BAND:] = (weight * s).astype(bf16)

    each_block(BAND_LO + iota((32, BAND), 1), base, store)


def front_kernel(ids, own_ref, peer_ref, fwd_ref, inv_ref, env_ref, e_ref):
    tm = ids[2]
    own = own_ref[pl.ds(2 * tm, 2)].reshape(64, HALF)
    peer = peer_ref[...].reshape(64, HALF)
    terms = jnp.dot(jnp.concatenate([own, peer], axis=0), fwd_ref[...], preferred_element_type=f32)
    col = lax.broadcasted_iota(jnp.int32, (1, 2 * BAND), 1)
    sign = (1 - 2 * (col & 1)).astype(f32)
    first = jnp.where(tm == 0, jnp.ones_like(sign), sign)
    second = jnp.where(tm == 0, sign, jnp.ones_like(sign))
    spectrum = terms[:64] * first + terms[64:] * second
    both = jnp.concatenate([spectrum, spectrum * sign], axis=0)
    re, im = both[:, :BAND], both[:, BAND:]
    real_form = jnp.concatenate([re, -im], axis=1)
    imag_form = jnp.concatenate([im, re], axis=1)
    forms = jnp.concatenate([real_form, imag_form], axis=0).astype(bf16)
    analytic = lax.dot_general(forms, inv_ref[...], (((1,), (1,)), ((), ())), preferred_element_type=f32)
    real, imag = analytic[:128], analytic[128:]
    energy = real * real + imag * imag
    sums = jnp.sum(energy, axis=1, keepdims=True)
    sums = sums[:64] + sums[64:]
    env = jnp.dot(energy.astype(bf16), env_ref[...], preferred_element_type=f32)
    lane = lax.broadcasted_iota(jnp.int32, (1, 2 * FB), 1)
    odd = (2 * (lane & 1) - 1).astype(f32)
    env = env[:64] + env[64:] * odd
    factor = 1.0 / (math.sqrt(SAMPLES) * (sums / SAMPLES + epsilon))
    e_ref[...] = (env * factor).astype(bf16)


def expand(normal, lhs):
    normal = normal.astype(f32)
    kept = (iota((FB, 128), 0) & 1) == (iota((FB, 128), 1) >> 6)
    for w in range(2):
        re = normal[32 * w : 32 * w + 32, :FB]
        im = normal[32 * w : 32 * w + 32, FB:]
        for part, quad in enumerate(((re, -im, re, -im), (im, re, im, re))):
            t = jnp.concatenate(quad, axis=0).T
            lhs[pl.ds(2 * w + part, FB, stride=4), :] = jnp.where(kept, t, 0.0)


def stack(delays, lhs, store):
    one = [half_turn((d - 512).astype(f32) * (math.pi / 1024)) for d in delays]
    two = [turn(v, v) for v in one]
    mid = two
    for i in range(FB // 4):
        powers, ahead = [[], [], [], []], []
        for (c, s), (c1, s1), v2 in zip(mid, one, two):
            cc, ss, cs, sc = c * c1, s * s1, c * s1, s * c1
            last = turn((c, s), v2)
            for group, v in zip(powers, ((cc + ss, sc - cs), (c, s), (cc - ss, sc + cs), last)):
                group.append([x.astype(bf16) for x in v])
            ahead.append(turn(last, v2))
        mid = ahead
        at = 16 * i
        a = jnp.concatenate([v[at : at + 16, :] for v in lhs], axis=1)
        for g in range(2):
            z = [x for even, odd in zip(powers[2 * g], powers[2 * g + 1]) for x in (*even, *odd)]
            r = jnp.dot(a, jnp.concatenate(z, axis=0), preferred_element_type=f32)
            store(at + 8 * g, r[8 * g : 8 * g + 8])


def near_kernel(own_d, core_d, own_e, core_e, acc_ref, wide, lhs):
    for i, e in enumerate((own_e, core_e)):
        expand(e[...], wide)
        lhs[i] = wide[...].astype(bf16)
    for j in range(2):

        def store(at, r):
            acc_ref[j, at : at + 8, :] = r

        stack((own_d[j], core_d[0, j]), (lhs.at[0], lhs.at[1]), store)


def far_kernel(far_d, far_e, acc_ref, out_ref, wide, lhs, acc):
    for i in range(2):
        expand(far_e[i], wide)
        lhs[i] = wide[...].astype(bf16)
    for j in range(2):

        def store(at, r):
            acc[at : at + 8, :] = acc_ref[j, at : at + 8, :] + r

        stack((far_d[0, j], far_d[1, j]), (lhs.at[0], lhs.at[1]), store)
        for q in range(4):
            out_ref[128 * j : 128 * j + 128, 128 * q : 128 * q + 128] = acc[pl.ds(q, FB, stride=4), :].T.astype(bf16)


def final_kernel(part_ref, q_ref, out_ref):
    total = part_ref[0:16, :].astype(f32)
    for i in range(1, 16):
        total = total + part_ref[16 * i : 16 * i + 16, :].astype(f32)
    total = total[:8] + total[8:]
    zero = jnp.zeros((8, TB), f32)
    for w in range(2):
        a = jnp.concatenate([*split(total[:, w * TB : (w + 1) * TB]), zero], axis=0).astype(bf16)
        r = [jnp.dot(a, q_ref[w, i], preferred_element_type=f32) for i in range(3)]
        out_ref[w] = (r[0][:8] + ((r[0][8:16] + r[1][:8]) + ((r[0][16:24] + r[1][8:16]) + r[2][:8])))


def call(kernel, outs, ins, scratch=(), limit=24):
    return pl.pallas_call(
        kernel,
        out_shape=outs,
        in_specs=ins,
        out_specs=jax.tree.map(lambda _: VMEM, outs),
        scratch_shapes=list(scratch),
        compiler_params=pltpu.CompilerParams(vmem_limit_bytes=limit << 20),
    )


def flip(v, *axes):
    n = 2 ** len(axes)
    return lax.ppermute(v, axes, [(i, n - 1 - i) for i in range(n)])


def shape(dims, dtype):
    return jax.ShapeDtypeStruct(dims, dtype)


def on_device(traces, delays, offsets):
    tm = lax.axis_index("tm")
    ids = jnp.stack([lax.axis_index(a) for a in ("xh", "core", "tm")]).astype(jnp.int32)
    rows = traces.transpose(1, 0, 2)
    send = jnp.where(tm == 0, rows[2:], rows[:2])
    send, ids = lax.optimization_barrier((send, ids))
    peer = flip(send, "tm")
    pair = shape((2, 32, 128), jnp.int32)
    mine, far, cross, fwd, env = call(
        first_kernel,
        (
            pair,
            pair,
            shape((2, 2, 32, 128), jnp.int32),
            shape((HALF, 2 * BAND), bf16),
            shape((HALF, 2 * FB), bf16),
        ),
        [SMEM, HBM],
        [
            pltpu.VMEM((32, 1024), jnp.int32),
            pltpu.VMEM((1024, 32), f32),
            pltpu.VMEM((2, 32, BAND + FB), f32),
            pltpu.SemaphoreType.DMA,
        ],
    )(ids, pltpu.with_memory_space_constraint(delays.T, pltpu.HBM))
    core_d = flip(cross, "core")
    inv = call(
        inverse_kernel, shape((HALF, 2 * BAND), bf16), [VMEM], [pltpu.VMEM((2, 32, BAND), f32)]
    )(mine)
    peer, core_d, inv = lax.optimization_barrier((peer, core_d, inv))
    e = call(front_kernel, shape((64, 2 * FB), bf16), [SMEM] + [VMEM] * 5)(ids, rows, peer, fwd, inv, env)
    far_d = flip(jnp.stack([far, core_d[1]]), "xh")
    core_e = flip(e, "core")
    far_e = flip(jnp.stack([e, core_e]), "xh")
    acc = call(
        near_kernel,
        shape((2, 512, 128), f32),
        [VMEM] * 4,
        [pltpu.VMEM((512, 128), f32), pltpu.VMEM((2, 512, 128), bf16)],
    )(mine, core_d, e, core_e)
    offsets, after = lax.optimization_barrier((offsets, acc[0, :8]))
    q = call(times_kernel, shape((2, 3, 2 * FB, TB), bf16), [SMEM, VMEM])(offsets, after)
    q, acc = lax.optimization_barrier((q, acc))
    part = call(
        far_kernel,
        shape((256, 512), bf16),
        [VMEM] * 3,
        [pltpu.VMEM((512, 128), f32), pltpu.VMEM((2, 512, 128), bf16), pltpu.VMEM((512, 128), f32)],
    )(far_d, far_e, acc)
    parts = lax.all_to_all(part.reshape(32, 8, 512), ("zh", "y", "xl"), 0, 0, tiled=True)
    return call(final_kernel, shape((2, 8, TB), f32), [VMEM] * 2)(parts.reshape(256, 512), q)


def solution(mesh):
    chan = ("xh", "xl", "zh", "y", "core")
    fine = Mesh(mesh.devices.reshape(2, 2, 4, 4, 2, 2), chan + ("tm",))
    placed = (P(chan, None, "tm"), P(None, chan), P("tm"))
    return jax.shard_map(
        on_device, mesh=fine, in_specs=placed, out_specs=P("tm", chan, None), check_vma=False
    )
```

```python
import math

import jax
import jax.numpy as jnp
from jax import lax
from jax.experimental import pallas as pl
from jax.experimental.pallas import tpu as pltpu
from jax.sharding import Mesh
from jax.sharding import PartitionSpec as P

SAMPLES = 2048
HALF = 1024
BAND = 512
FB = 128
TB = 256
BAND_LO = 128
DEC = 8
CHANNELS = 4096
epsilon = 1e-06
bf16 = jnp.bfloat16
f32 = jnp.float32
VMEM = pl.BlockSpec(memory_space=pltpu.VMEM)
SMEM = pl.BlockSpec(memory_space=pltpu.SMEM)
HBM = pl.BlockSpec(memory_space=pltpu.HBM)


def half_turn(u):
    v = u * u
    s = 1.0 + v * (-1 / 6 + v * (1 / 120 + v * (-1 / 5040 + v * (1 / 362880 + v * (-1 / 39916800)))))
    c = 1.0 + v * (
        -1 / 2 + v * (1 / 24 + v * (-1 / 720 + v * (1 / 40320 + v * (-1 / 3628800 + v * (1 / 479001600)))))
    )
    return -(u * s), c


def circle(p):
    c, s = half_turn(((p & (SAMPLES - 1)) - HALF).astype(f32) * (math.pi / SAMPLES))
    return c * c - s * s, 2.0 * c * s


def iota(dims, axis):
    return lax.broadcasted_iota(jnp.int32, dims, axis)


def turn(u, v):
    return u[0] * v[0] - u[1] * v[1], u[0] * v[1] + u[1] * v[0]


def each_block(freq, base, store):
    step = iota(freq.shape, 0) * freq
    base[0], base[1] = circle(32 * step)
    low = circle(step)

    def body(a, _):
        at = pl.ds(pl.multiple_of(32 * a, 32), 32)
        store(at, *turn((base[0, pl.ds(a, 1), :], base[1, pl.ds(a, 1), :]), low))
        return 0

    lax.fori_loop(0, 32, body, 0, unroll=2)


def first_kernel(ids, d_hbm, mine, far, cross, fwd_ref, env_ref, d_ref, rows, base, sem):
    copy = pltpu.make_async_copy(d_hbm, d_ref, sem)
    copy.start()
    lane = iota((32, BAND + FB), 1)

    def store(at, c, s):
        fwd_ref[at, :BAND] = c[:, :BAND].astype(bf16)
        fwd_ref[at, BAND:] = (-s[:, :BAND]).astype(bf16)
        env_ref[at, :FB] = c[:, BAND:].astype(bf16)
        env_ref[at, FB:] = (-s[:, BAND:]).astype(bf16)

    each_block(jnp.where(lane < BAND, BAND_LO + lane, lane - BAND + 1), base, store)
    copy.wait()
    xh, core = ids[0], ids[1]
    for m in range(8):
        rows[pl.ds(128 * m, 128), :] = d_ref[:, pl.ds(128 * m, 128)].astype(f32).T

    def nodes(h, b, j):
        parts = []
        for zh in (2 * j, 2 * j + 1):
            for y in range(4):
                for xl in range(2):
                    x = 2 * (xh ^ h) + xl
                    at = pl.multiple_of((((x * 4 + zh) * 4 + y) * 2 + (core ^ b)) * 8, 8)
                    parts.append(rows[pl.ds(at, 8), :])
        return jnp.concatenate(parts, axis=0).T.astype(jnp.int32)

    for j in range(2):
        mine[j] = nodes(0, 0, j)
        far[j] = nodes(1, 0, j).astype(jnp.int16)
        for h in range(2):
            cross[h, j] = nodes(h, 1, j).astype(jnp.int16)


def split(v):
    high = v.astype(bf16).astype(f32)
    middle = (v - high).astype(bf16).astype(f32)
    return high, middle, (v - high) - middle


def times_kernel(offs, after, q_ref):
    scale = 1.0 / math.sqrt(FB * CHANNELS)
    for w in range(2):
        c, s = circle((1 + iota((FB, TB), 0)) * (DEC * iota((FB, TB), 1) + offs[w]))
        for i, (re, im) in enumerate(zip(split(c * scale), split(s * -scale))):
            q_ref[w, i, :FB] = re.astype(bf16)
            q_ref[w, i, FB:] = im.astype(bf16)


def inverse_kernel(after, inv_ref, base):
    _, taper = circle(2 * iota((1, BAND), 1) + 1)
    weight = taper * taper * (2.0 / SAMPLES)

    def store(at, c, s):
        inv_ref[at, :BAND] = (weight * c).astype(bf16)
        inv_ref[at, BAND:] = (weight * s).astype(bf16)

    each_block(BAND_LO + iota((32, BAND), 1), base, store)


def front_kernel(ids, own_ref, peer_ref, fwd_ref, inv_ref, env_ref, e_ref):
    tm = ids[2]
    own = own_ref[pl.ds(2 * tm, 2)].reshape(64, HALF)
    peer = peer_ref[...].reshape(64, HALF)
    terms = jnp.dot(jnp.concatenate([own, peer], axis=0), fwd_ref[...], preferred_element_type=f32)
    col = lax.broadcasted_iota(jnp.int32, (1, 2 * BAND), 1)
    sign = (1 - 2 * (col & 1)).astype(f32)
    first = jnp.where(tm == 0, jnp.ones_like(sign), sign)
    second = jnp.where(tm == 0, sign, jnp.ones_like(sign))
    spectrum = terms[:64] * first + terms[64:] * second
    both = jnp.concatenate([spectrum, spectrum * sign], axis=0)
    re, im = both[:, :BAND], both[:, BAND:]
    real_form = jnp.concatenate([re, -im], axis=1)
    imag_form = jnp.concatenate([im, re], axis=1)
    forms = jnp.concatenate([real_form, imag_form], axis=0).astype(bf16)
    analytic = lax.dot_general(forms, inv_ref[...], (((1,), (1,)), ((), ())), preferred_element_type=f32)
    real, imag = analytic[:128], analytic[128:]
    energy = real * real + imag * imag
    sums = jnp.sum(energy, axis=1, keepdims=True)
    sums = sums[:64] + sums[64:]
    env = jnp.dot(energy.astype(bf16), env_ref[...], preferred_element_type=f32)
    lane = lax.broadcasted_iota(jnp.int32, (1, 2 * FB), 1)
    odd = (2 * (lane & 1) - 1).astype(f32)
    env = env[:64] + env[64:] * odd
    factor = 1.0 / (math.sqrt(SAMPLES) * (sums / SAMPLES + epsilon))
    e_ref[...] = (env * factor).astype(bf16)


def expand(normal, lhs):
    normal = normal.astype(f32)
    kept = (iota((FB, 128), 0) & 1) == (iota((FB, 128), 1) >> 6)
    for w in range(2):
        re = normal[32 * w : 32 * w + 32, :FB]
        im = normal[32 * w : 32 * w + 32, FB:]
        for part, quad in enumerate(((re, -im, re, -im), (im, re, im, re))):
            t = jnp.concatenate(quad, axis=0).T
            lhs[pl.ds(2 * w + part, FB, stride=4), :] = jnp.where(kept, t, 0.0)


def stack(delays, lhs, store):
    one = [half_turn((d.astype(jnp.int32) - 512).astype(f32) * (math.pi / 1024)) for d in delays]
    two = [turn(v, v) for v in one]
    mid = two
    for i in range(FB // 4):
        powers, ahead = [[], [], [], []], []
        for (c, s), (c1, s1), v2 in zip(mid, one, two):
            cc, ss, cs, sc = c * c1, s * s1, c * s1, s * c1
            last = turn((c, s), v2)
            for group, v in zip(powers, ((cc + ss, sc - cs), (c, s), (cc - ss, sc + cs), last)):
                group.append([x.astype(bf16) for x in v])
            ahead.append(turn(last, v2))
        mid = ahead
        at = 16 * i
        a = jnp.concatenate([v[at : at + 16, :] for v in lhs], axis=1)
        for g in range(2):
            z = [x for even, odd in zip(powers[2 * g], powers[2 * g + 1]) for x in (*even, *odd)]
            r = jnp.dot(a, jnp.concatenate(z, axis=0), preferred_element_type=f32)
            store(at + 8 * g, r[8 * g : 8 * g + 8])


def near_kernel(own_d, core_d, own_e, core_e, acc_ref, wide, lhs):
    for i, e in enumerate((own_e, core_e)):
        expand(e[...], wide)
        lhs[i] = wide[...].astype(bf16)
    for j in range(2):

        def store(at, r):
            acc_ref[j, at : at + 8, :] = r

        stack((own_d[j], core_d[0, j]), (lhs.at[0], lhs.at[1]), store)


def far_kernel(far_d, far_e, acc_ref, out_ref, wide, lhs, acc):
    for i in range(2):
        expand(far_e[i], wide)
        lhs[i] = wide[...].astype(bf16)
    for j in range(2):

        def store(at, r):
            acc[at : at + 8, :] = acc_ref[j, at : at + 8, :] + r

        stack((far_d[0, j], far_d[1, j]), (lhs.at[0], lhs.at[1]), store)
        for q in range(4):
            out_ref[128 * j : 128 * j + 128, 128 * q : 128 * q + 128] = acc[pl.ds(q, FB, stride=4), :].T.astype(bf16)


def final_kernel(part_ref, q_ref, out_ref):
    total = part_ref[0:16, :].astype(f32)
    for i in range(1, 16):
        total = total + part_ref[16 * i : 16 * i + 16, :].astype(f32)
    total = total[:8] + total[8:]
    zero = jnp.zeros((8, TB), f32)
    for w in range(2):
        a = jnp.concatenate([*split(total[:, w * TB : (w + 1) * TB]), zero], axis=0).astype(bf16)
        r = [jnp.dot(a, q_ref[w, i], preferred_element_type=f32) for i in range(3)]
        out_ref[w] = (r[0][:8] + ((r[0][8:16] + r[1][:8]) + ((r[0][16:24] + r[1][8:16]) + r[2][:8])))


def call(kernel, outs, ins, scratch=(), limit=24):
    return pl.pallas_call(
        kernel,
        out_shape=outs,
        in_specs=ins,
        out_specs=jax.tree.map(lambda _: VMEM, outs),
        scratch_shapes=list(scratch),
        compiler_params=pltpu.CompilerParams(vmem_limit_bytes=limit << 20),
    )


def flip(v, *axes):
    n = 2 ** len(axes)
    return lax.ppermute(v, axes, [(i, n - 1 - i) for i in range(n)])


def shape(dims, dtype):
    return jax.ShapeDtypeStruct(dims, dtype)


def on_device(traces, delays, offsets):
    tm = lax.axis_index("tm")
    ids = jnp.stack([lax.axis_index(a) for a in ("xh", "core", "tm")]).astype(jnp.int32)
    rows = traces.transpose(1, 0, 2)
    send = jnp.where(tm == 0, rows[2:], rows[:2])
    send, ids = lax.optimization_barrier((send, ids))
    peer = flip(send, "tm")
    mine, far, cross, fwd, env = call(
        first_kernel,
        (
            shape((2, 32, 128), jnp.int32),
            shape((2, 32, 128), jnp.int16),
            shape((2, 2, 32, 128), jnp.int16),
            shape((HALF, 2 * BAND), bf16),
            shape((HALF, 2 * FB), bf16),
        ),
        [SMEM, HBM],
        [
            pltpu.VMEM((32, 1024), jnp.int32),
            pltpu.VMEM((1024, 32), f32),
            pltpu.VMEM((2, 32, BAND + FB), f32),
            pltpu.SemaphoreType.DMA,
        ],
    )(ids, pltpu.with_memory_space_constraint(delays.T, pltpu.HBM))
    core_d = flip(cross, "core")
    inv = call(
        inverse_kernel, shape((HALF, 2 * BAND), bf16), [VMEM], [pltpu.VMEM((2, 32, BAND), f32)]
    )(mine)
    peer, core_d, inv = lax.optimization_barrier((peer, core_d, inv))
    e = call(front_kernel, shape((64, 2 * FB), bf16), [SMEM] + [VMEM] * 5)(ids, rows, peer, fwd, inv, env)
    far_d = flip(jnp.stack([far, core_d[1]]), "xh")
    core_e = flip(e, "core")
    far_e = flip(jnp.stack([e, core_e]), "xh")
    acc = call(
        near_kernel,
        shape((2, 512, 128), f32),
        [VMEM] * 4,
        [pltpu.VMEM((512, 128), f32), pltpu.VMEM((2, 512, 128), bf16)],
    )(mine, core_d, e, core_e)
    offsets, after = lax.optimization_barrier((offsets, acc[0, :8]))
    q = call(times_kernel, shape((2, 3, 2 * FB, TB), bf16), [SMEM, VMEM])(offsets, after)
    q, acc = lax.optimization_barrier((q, acc))
    part = call(
        far_kernel,
        shape((256, 512), bf16),
        [VMEM] * 3,
        [pltpu.VMEM((512, 128), f32), pltpu.VMEM((2, 512, 128), bf16), pltpu.VMEM((512, 128), f32)],
    )(far_d, far_e, acc)
    parts = lax.all_to_all(part.reshape(32, 8, 512), ("zh", "y", "xl"), 0, 0, tiled=True)
    return call(final_kernel, shape((2, 8, TB), f32), [VMEM] * 2)(parts.reshape(256, 512), q)


def solution(mesh):
    chan = ("xh", "xl", "zh", "y", "core")
    fine = Mesh(mesh.devices.reshape(2, 2, 4, 4, 2, 2), chan + ("tm",))
    placed = (P(chan, None, "tm"), P(None, chan), P("tm"))
    return jax.shard_map(
        on_device, mesh=fine, in_specs=placed, out_specs=P("tm", chan, None), check_vma=False
    )
```

```python
import math

import jax
import jax.numpy as jnp
from jax import lax
from jax.experimental import pallas as pl
from jax.experimental.pallas import tpu as pltpu
from jax.sharding import Mesh
from jax.sharding import PartitionSpec as P

SAMPLES = 2048
HALF = 1024
BAND = 512
FB = 128
TB = 256
BAND_LO = 128
DEC = 8
CHANNELS = 4096
epsilon = 1e-06
bf16 = jnp.bfloat16
f32 = jnp.float32
VMEM = pl.BlockSpec(memory_space=pltpu.VMEM)
SMEM = pl.BlockSpec(memory_space=pltpu.SMEM)
HBM = pl.BlockSpec(memory_space=pltpu.HBM)


def half_turn(u):
    v = u * u
    s = 1.0 + v * (-1 / 6 + v * (1 / 120 + v * (-1 / 5040 + v * (1 / 362880 + v * (-1 / 39916800)))))
    c = 1.0 + v * (
        -1 / 2 + v * (1 / 24 + v * (-1 / 720 + v * (1 / 40320 + v * (-1 / 3628800 + v * (1 / 479001600)))))
    )
    return -(u * s), c


def circle(p):
    c, s = half_turn(((p & (SAMPLES - 1)) - HALF).astype(f32) * (math.pi / SAMPLES))
    return c * c - s * s, 2.0 * c * s


def iota(dims, axis):
    return lax.broadcasted_iota(jnp.int32, dims, axis)


def turn(u, v):
    return u[0] * v[0] - u[1] * v[1], u[0] * v[1] + u[1] * v[0]


def each_block(freq, base, store):
    step = iota(freq.shape, 0) * freq
    base[0], base[1] = circle(32 * step)
    low = circle(step)

    def body(a, _):
        at = pl.ds(pl.multiple_of(32 * a, 32), 32)
        store(at, *turn((base[0, pl.ds(a, 1), :], base[1, pl.ds(a, 1), :]), low))
        return 0

    lax.fori_loop(0, 32, body, 0, unroll=2)


def first_kernel(ids, d_hbm, mine, cross, fwd_ref, env_ref, d_ref, rows, base, sem):
    copy = pltpu.make_async_copy(d_hbm, d_ref, sem)
    copy.start()
    lane = iota((32, BAND + FB), 1)

    def store(at, c, s):
        fwd_ref[at, :BAND] = c[:, :BAND].astype(bf16)
        fwd_ref[at, BAND:] = (-s[:, :BAND]).astype(bf16)
        env_ref[at, :FB] = c[:, BAND:].astype(bf16)
        env_ref[at, FB:] = (-s[:, BAND:]).astype(bf16)

    each_block(jnp.where(lane < BAND, BAND_LO + lane, lane - BAND + 1), base, store)
    copy.wait()
    core = ids[1]
    for m in range(8):
        rows[pl.ds(128 * m, 128), :] = d_ref[:, pl.ds(128 * m, 128)].astype(f32).T

    def nodes(b, x):
        parts = []
        for y in range(4):
            for zh in range(4):
                at = pl.multiple_of((((x * 4 + zh) * 4 + y) * 2 + (core ^ b)) * 8, 8)
                parts.append(rows[pl.ds(at, 8), :])
        return jnp.concatenate(parts, axis=0).T.astype(jnp.int32)

    for x in range(4):
        mine[x] = nodes(0, x)
        cross[x] = nodes(1, x).astype(jnp.int16)


def split(v):
    high = v.astype(bf16).astype(f32)
    middle = (v - high).astype(bf16).astype(f32)
    return high, middle, (v - high) - middle


def times_kernel(offs, after, q_ref):
    scale = 1.0 / math.sqrt(FB * CHANNELS)
    for w in range(2):
        c, s = circle((1 + iota((FB, TB), 0)) * (DEC * iota((FB, TB), 1) + offs[w]))
        for i, (re, im) in enumerate(zip(split(c * scale), split(s * -scale))):
            q_ref[w, i, :FB] = re.astype(bf16)
            q_ref[w, i, FB:] = im.astype(bf16)


def inverse_kernel(after, inv_ref, base):
    _, taper = circle(2 * iota((1, BAND), 1) + 1)
    weight = taper * taper * (2.0 / SAMPLES)

    def store(at, c, s):
        inv_ref[at, :BAND] = (weight * c).astype(bf16)
        inv_ref[at, BAND:] = (weight * s).astype(bf16)

    each_block(BAND_LO + iota((32, BAND), 1), base, store)


def front_kernel(ids, own_ref, peer_ref, fwd_ref, inv_ref, env_ref, e_ref):
    tm = ids[2]
    own = own_ref[pl.ds(2 * tm, 2)].reshape(64, HALF)
    peer = peer_ref[...].reshape(64, HALF)
    terms = jnp.dot(jnp.concatenate([own, peer], axis=0), fwd_ref[...], preferred_element_type=f32)
    col = lax.broadcasted_iota(jnp.int32, (1, 2 * BAND), 1)
    sign = (1 - 2 * (col & 1)).astype(f32)
    first = jnp.where(tm == 0, jnp.ones_like(sign), sign)
    second = jnp.where(tm == 0, sign, jnp.ones_like(sign))
    spectrum = terms[:64] * first + terms[64:] * second
    both = jnp.concatenate([spectrum, spectrum * sign], axis=0)
    re, im = both[:, :BAND], both[:, BAND:]
    real_form = jnp.concatenate([re, -im], axis=1)
    imag_form = jnp.concatenate([im, re], axis=1)
    forms = jnp.concatenate([real_form, imag_form], axis=0).astype(bf16)
    analytic = lax.dot_general(forms, inv_ref[...], (((1,), (1,)), ((), ())), preferred_element_type=f32)
    real, imag = analytic[:128], analytic[128:]
    energy = real * real + imag * imag
    sums = jnp.sum(energy, axis=1, keepdims=True)
    sums = sums[:64] + sums[64:]
    env = jnp.dot(energy.astype(bf16), env_ref[...], preferred_element_type=f32)
    lane = lax.broadcasted_iota(jnp.int32, (1, 2 * FB), 1)
    odd = (2 * (lane & 1) - 1).astype(f32)
    env = env[:64] + env[64:] * odd
    factor = 1.0 / (math.sqrt(SAMPLES) * (sums / SAMPLES + epsilon))
    e_ref[...] = (env * factor).astype(bf16)


def expand(normal, lhs):
    normal = normal.astype(f32)
    kept = (iota((FB, 128), 0) & 1) == (iota((FB, 128), 1) >> 6)
    for w in range(2):
        re = normal[32 * w : 32 * w + 32, :FB]
        im = normal[32 * w : 32 * w + 32, FB:]
        for part, quad in enumerate(((re, -im, re, -im), (im, re, im, re))):
            t = jnp.concatenate(quad, axis=0).T
            lhs[pl.ds(2 * w + part, FB, stride=4), :] = jnp.where(kept, t, 0.0)


def stack(delays, lhs, store):
    one = [half_turn((d.astype(jnp.int32) - 512).astype(f32) * (math.pi / 1024)) for d in delays]
    two = [turn(v, v) for v in one]
    mid = two
    for i in range(FB // 4):
        powers, ahead = [[], [], [], []], []
        for (c, s), (c1, s1), v2 in zip(mid, one, two):
            cc, ss, cs, sc = c * c1, s * s1, c * s1, s * c1
            last = turn((c, s), v2)
            for group, v in zip(powers, ((cc + ss, sc - cs), (c, s), (cc - ss, sc + cs), last)):
                group.append([x.astype(bf16) for x in v])
            ahead.append(turn(last, v2))
        mid = ahead
        at = 16 * i
        a = jnp.concatenate([v[at : at + 16, :] for v in lhs], axis=1)
        for g in range(2):
            z = [x for even, odd in zip(powers[2 * g], powers[2 * g + 1]) for x in (*even, *odd)]
            r = jnp.dot(a, jnp.concatenate(z, axis=0), preferred_element_type=f32)
            store(at + 8 * g, r[8 * g : 8 * g + 8])


def stack_kernel(own_d, core_d, own_e, core_e, out_ref, wide, lhs, acc):
    for i, e in enumerate((own_e, core_e)):
        expand(e[...], wide)
        lhs[i] = wide[...].astype(bf16)
    for x in range(4):

        def store(at, r):
            acc[x % 2, at : at + 8, :] = r

        stack((own_d[x], core_d[x]), (lhs.at[0], lhs.at[1]), store)
        for q in range(4):
            part = acc[x % 2, pl.ds(q, FB, stride=4), :].T
            out_ref[128 * x : 128 * x + 128, 128 * q : 128 * q + 128] = part.astype(bf16)


def plane_kernel(ids, part_ref, o0, o1, o2, o3, acc):
    total = part_ref[0:32, :].astype(f32)
    for i in range(1, 16):
        total = total + part_ref[32 * i : 32 * i + 32, :].astype(f32)
    acc[...] = total
    for k, out in enumerate((o0, o1, o2, o3)):
        out[...] = acc[pl.ds(pl.multiple_of(8 * ((ids[0] + k) & 3), 8), 8), :]


def final_kernel(p0, p1, p2, p3, q_ref, out_ref):
    total = (p0[...] + p1[...]) + (p2[...] + p3[...])
    zero = jnp.zeros((8, TB), f32)
    for w in range(2):
        a = jnp.concatenate([*split(total[:, w * TB : (w + 1) * TB]), zero], axis=0).astype(bf16)
        r = [jnp.dot(a, q_ref[w, i], preferred_element_type=f32) for i in range(3)]
        out_ref[w] = (r[0][:8] + ((r[0][8:16] + r[1][:8]) + ((r[0][16:24] + r[1][8:16]) + r[2][:8])))


def call(kernel, outs, ins, scratch=(), limit=24):
    return pl.pallas_call(
        kernel,
        out_shape=outs,
        in_specs=ins,
        out_specs=jax.tree.map(lambda _: VMEM, outs),
        scratch_shapes=list(scratch),
        compiler_params=pltpu.CompilerParams(vmem_limit_bytes=limit << 20),
    )


def flip(v, *axes):
    n = 2 ** len(axes)
    return lax.ppermute(v, axes, [(i, n - 1 - i) for i in range(n)])


def shift(v, axis, k):
    n = lax.axis_size(axis)
    return lax.ppermute(v, axis, [(i, (i + k) % n) for i in range(n)])


def shape(dims, dtype):
    return jax.ShapeDtypeStruct(dims, dtype)


def on_device(traces, delays, offsets):
    tm = lax.axis_index("tm")
    ids = jnp.stack([lax.axis_index(a) for a in ("zh", "core", "tm")]).astype(jnp.int32)
    rows = traces.transpose(1, 0, 2)
    send = jnp.where(tm == 0, rows[2:], rows[:2])
    send, ids = lax.optimization_barrier((send, ids))
    peer = flip(send, "tm")
    mine, cross, fwd, env = call(
        first_kernel,
        (
            shape((4, 32, 128), jnp.int32),
            shape((4, 32, 128), jnp.int16),
            shape((HALF, 2 * BAND), bf16),
            shape((HALF, 2 * FB), bf16),
        ),
        [SMEM, HBM],
        [
            pltpu.VMEM((32, 1024), jnp.int32),
            pltpu.VMEM((1024, 32), f32),
            pltpu.VMEM((2, 32, BAND + FB), f32),
            pltpu.SemaphoreType.DMA,
        ],
    )(ids, pltpu.with_memory_space_constraint(delays.T, pltpu.HBM))
    core_d = flip(cross, "core")
    inv = call(
        inverse_kernel, shape((HALF, 2 * BAND), bf16), [VMEM], [pltpu.VMEM((2, 32, BAND), f32)]
    )(mine)
    peer, core_d, inv = lax.optimization_barrier((peer, core_d, inv))
    e = call(front_kernel, shape((64, 2 * FB), bf16), [SMEM] + [VMEM] * 5)(ids, rows, peer, fwd, inv, env)
    core_e = flip(e, "core")
    part = call(
        stack_kernel,
        shape((512, 512), bf16),
        [VMEM] * 4,
        [pltpu.VMEM((512, 128), f32), pltpu.VMEM((2, 512, 128), bf16), pltpu.VMEM((2, 512, 128), f32)],
    )(mine, core_d, e, core_e)
    parts = lax.all_to_all(part.reshape(16, 32, 512), ("x", "y"), 0, 0, tiled=True)
    nodes = shape((8, 512), f32)
    planes = call(plane_kernel, (nodes,) * 4, [SMEM, VMEM], [pltpu.VMEM((32, 512), f32)])(ids, parts.reshape(512, 512))
    got = [planes[0]] + [shift(planes[k], "zh", k) for k in (1, 2, 3)]
    offsets, after = lax.optimization_barrier((offsets, planes[0]))
    q = call(times_kernel, shape((2, 3, 2 * FB, TB), bf16), [SMEM, VMEM])(offsets, after)
    return call(final_kernel, shape((2, 8, TB), f32), [VMEM] * 5)(*got, q)


def solution(mesh):
    chan = ("x", "zh", "y", "core")
    fine = Mesh(mesh.devices.reshape(4, 4, 4, 2, 2), chan + ("tm",))
    placed = (P(chan, None, "tm"), P(None, chan), P("tm"))
    return jax.shard_map(
        on_device, mesh=fine, in_specs=placed, out_specs=P("tm", chan, None), check_vma=False
    )
```

```python
import math

import jax
import jax.numpy as jnp
from jax import lax
from jax.experimental import pallas as pl
from jax.experimental.pallas import tpu as pltpu
from jax.sharding import Mesh
from jax.sharding import PartitionSpec as P

SAMPLES = 2048
HALF = 1024
BAND = 512
FB = 128
TB = 256
BAND_LO = 128
DEC = 8
CHANNELS = 4096
epsilon = 1e-06
bf16 = jnp.bfloat16
f32 = jnp.float32
VMEM = pl.BlockSpec(memory_space=pltpu.VMEM)
SMEM = pl.BlockSpec(memory_space=pltpu.SMEM)
HBM = pl.BlockSpec(memory_space=pltpu.HBM)


def half_turn(u):
    v = u * u
    s = 1.0 + v * (-1 / 6 + v * (1 / 120 + v * (-1 / 5040 + v * (1 / 362880 + v * (-1 / 39916800)))))
    c = 1.0 + v * (
        -1 / 2 + v * (1 / 24 + v * (-1 / 720 + v * (1 / 40320 + v * (-1 / 3628800 + v * (1 / 479001600)))))
    )
    return -(u * s), c


def circle(p):
    c, s = half_turn(((p & (SAMPLES - 1)) - HALF).astype(f32) * (math.pi / SAMPLES))
    return c * c - s * s, 2.0 * c * s


def iota(dims, axis):
    return lax.broadcasted_iota(jnp.int32, dims, axis)


def turn(u, v):
    return u[0] * v[0] - u[1] * v[1], u[0] * v[1] + u[1] * v[0]


def each_block(freq, base, store):
    step = iota(freq.shape, 0) * freq
    base[0], base[1] = circle(32 * step)
    low = circle(step)

    def body(a, _):
        at = pl.ds(pl.multiple_of(32 * a, 32), 32)
        store(at, *turn((base[0, pl.ds(a, 1), :], base[1, pl.ds(a, 1), :]), low))
        return 0

    lax.fori_loop(0, 32, body, 0, unroll=2)


def band(lane):
    return BAND_LO + 2 * (lane & (BAND // 2 - 1)) + (lane >> 8)


def store_band(ref, at, c, s):
    h = BAND // 2
    for i in range(2):
        ref[at, 2 * h * i : 2 * h * i + h] = c[:, h * i : h * i + h].astype(bf16)
        ref[at, 2 * h * i + h : 2 * h * i + 2 * h] = s[:, h * i : h * i + h].astype(bf16)


def first_kernel(ids, d_hbm, mine, far, cross, fwd_ref, env_ref, d_ref, rows, base, sem):
    copy = pltpu.make_async_copy(d_hbm, d_ref, sem)
    copy.start()
    lane = iota((32, BAND + FB), 1)

    def store(at, c, s):
        store_band(fwd_ref, at, c[:, :BAND], -s[:, :BAND])
        env_ref[at, :FB] = c[:, BAND:].astype(bf16)
        env_ref[at, FB:] = (-s[:, BAND:]).astype(bf16)

    each_block(jnp.where(lane < BAND, band(lane & (BAND - 1)), lane - BAND + 1), base, store)
    copy.wait()
    xh, core = ids[0], ids[1]
    for m in range(8):
        rows[pl.ds(128 * m, 128), :] = d_ref[:, pl.ds(128 * m, 128)].astype(f32).T

    def nodes(h, b, j):
        parts = []
        for zh in (2 * j, 2 * j + 1):
            for y in range(4):
                for xl in range(2):
                    x = 2 * (xh ^ h) + xl
                    at = pl.multiple_of((((x * 4 + zh) * 4 + y) * 2 + (core ^ b)) * 8, 8)
                    parts.append(rows[pl.ds(at, 8), :])
        return jnp.concatenate(parts, axis=0).T.astype(jnp.int32)

    for j in range(2):
        mine[j] = nodes(0, 0, j)
        far[j] = nodes(1, 0, j).astype(jnp.int16)
        for h in range(2):
            cross[h, j] = nodes(h, 1, j).astype(jnp.int16)


def split(v):
    high = v.astype(bf16).astype(f32)
    middle = (v - high).astype(bf16).astype(f32)
    return high, middle, (v - high) - middle


def times_kernel(offs, after, q_ref):
    scale = 1.0 / math.sqrt(FB * CHANNELS)
    for w in range(2):
        c, s = circle((1 + iota((FB, TB), 0)) * (DEC * iota((FB, TB), 1) + offs[w]))
        for i, (re, im) in enumerate(zip(split(c * scale), split(s * -scale))):
            q_ref[w, i, :FB] = re.astype(bf16)
            q_ref[w, i, FB:] = im.astype(bf16)


def inverse_kernel(after, inv_ref, base):
    _, taper = circle(2 * (band(iota((1, BAND), 1)) - BAND_LO) + 1)
    weight = taper * taper * (2.0 / SAMPLES)

    def store(at, c, s):
        store_band(inv_ref, at, weight * c, weight * s)

    each_block(band(iota((32, BAND), 1)), base, store)


def front_kernel(ids, own_ref, peer_ref, fwd_ref, inv_ref, env_ref, e_ref):
    tm = ids[2]
    own = own_ref[pl.ds(2 * tm, 2)].reshape(64, HALF)
    peer = peer_ref[...].reshape(64, HALF)
    terms = jnp.dot(jnp.concatenate([own, peer], axis=0), fwd_ref[...], preferred_element_type=f32)
    even = terms[:64, :BAND] + terms[64:, :BAND]
    odd = (terms[:64, BAND:] - terms[64:, BAND:]) * jnp.where(tm == 0, 1.0, -1.0)
    halves = []
    for i, v in enumerate((even, odd)):
        re, im = v[:, : BAND // 2], v[:, BAND // 2 :]
        forms = jnp.concatenate(
            [jnp.concatenate([re, -im], axis=1), jnp.concatenate([im, re], axis=1)], axis=0
        ).astype(bf16)
        table = inv_ref[:, BAND * i : BAND * (i + 1)]
        halves.append(lax.dot_general(forms, table, (((1,), (1,)), ((), ())), preferred_element_type=f32))
    first, second = halves[0] + halves[1], halves[0] - halves[1]
    energy = jnp.concatenate([v[:64] * v[:64] + v[64:] * v[64:] for v in (first, second)], axis=0)
    sums = jnp.sum(energy, axis=1, keepdims=True)
    sums = sums[:64] + sums[64:]
    env = jnp.dot(energy.astype(bf16), env_ref[...], preferred_element_type=f32)
    lane = lax.broadcasted_iota(jnp.int32, (1, 2 * FB), 1)
    flip_sign = (2 * (lane & 1) - 1).astype(f32)
    env = env[:64] + env[64:] * flip_sign
    factor = 1.0 / (math.sqrt(SAMPLES) * (sums / SAMPLES + epsilon))
    e_ref[...] = (env * factor).astype(bf16)


def expand(normal, lhs):
    normal = normal.astype(f32)
    kept = (iota((FB, 128), 0) & 1) == (iota((FB, 128), 1) >> 6)
    for w in range(2):
        re = normal[32 * w : 32 * w + 32, :FB]
        im = normal[32 * w : 32 * w + 32, FB:]
        for part, quad in enumerate(((re, -im, re, -im), (im, re, im, re))):
            t = jnp.concatenate(quad, axis=0).T
            lhs[pl.ds(2 * w + part, FB, stride=4), :] = jnp.where(kept, t, 0.0)


def stack(delays, lhs, store):
    one = [half_turn((d.astype(jnp.int32) - 512).astype(f32) * (math.pi / 1024)) for d in delays]
    two = [turn(v, v) for v in one]
    mid = two
    for i in range(FB // 4):
        powers, ahead = [[], [], [], []], []
        for (c, s), (c1, s1), v2 in zip(mid, one, two):
            cc, ss, cs, sc = c * c1, s * s1, c * s1, s * c1
            last = turn((c, s), v2)
            for group, v in zip(powers, ((cc + ss, sc - cs), (c, s), (cc - ss, sc + cs), last)):
                group.append([x.astype(bf16) for x in v])
            ahead.append(turn(last, v2))
        mid = ahead
        at = 16 * i
        a = jnp.concatenate([v[at : at + 16, :] for v in lhs], axis=1)
        for g in range(2):
            z = [x for even, odd in zip(powers[2 * g], powers[2 * g + 1]) for x in (*even, *odd)]
            r = jnp.dot(a, jnp.concatenate(z, axis=0), preferred_element_type=f32)
            store(at + 8 * g, r[8 * g : 8 * g + 8])


def near_kernel(own_d, core_d, own_e, core_e, acc_ref, wide, lhs):
    for i, e in enumerate((own_e, core_e)):
        expand(e[...], wide)
        lhs[i] = wide[...].astype(bf16)
    for j in range(2):

        def store(at, r):
            acc_ref[j, at : at + 8, :] = r

        stack((own_d[j], core_d[0, j]), (lhs.at[0], lhs.at[1]), store)


def far_kernel(far_d, far_e, acc_ref, out_ref, wide, lhs, acc):
    for i in range(2):
        expand(far_e[i], wide)
        lhs[i] = wide[...].astype(bf16)
    for j in range(2):

        def store(at, r):
            acc[at : at + 8, :] = acc_ref[j, at : at + 8, :] + r

        stack((far_d[0, j], far_d[1, j]), (lhs.at[0], lhs.at[1]), store)
        for q in range(4):
            out_ref[128 * j : 128 * j + 128, 128 * q : 128 * q + 128] = acc[pl.ds(q, FB, stride=4), :].T.astype(bf16)


def final_kernel(part_ref, q_ref, out_ref):
    total = part_ref[0:16, :].astype(f32)
    for i in range(1, 16):
        total = total + part_ref[16 * i : 16 * i + 16, :].astype(f32)
    total = total[:8] + total[8:]
    zero = jnp.zeros((8, TB), f32)
    for w in range(2):
        a = jnp.concatenate([*split(total[:, w * TB : (w + 1) * TB]), zero], axis=0).astype(bf16)
        r = [jnp.dot(a, q_ref[w, i], preferred_element_type=f32) for i in range(3)]
        out_ref[w] = (r[0][:8] + ((r[0][8:16] + r[1][:8]) + ((r[0][16:24] + r[1][8:16]) + r[2][:8])))


def call(kernel, outs, ins, scratch=(), limit=24):
    return pl.pallas_call(
        kernel,
        out_shape=outs,
        in_specs=ins,
        out_specs=jax.tree.map(lambda _: VMEM, outs),
        scratch_shapes=list(scratch),
        compiler_params=pltpu.CompilerParams(vmem_limit_bytes=limit << 20),
    )


def flip(v, *axes):
    n = 2 ** len(axes)
    return lax.ppermute(v, axes, [(i, n - 1 - i) for i in range(n)])


def shape(dims, dtype):
    return jax.ShapeDtypeStruct(dims, dtype)


def on_device(traces, delays, offsets):
    tm = lax.axis_index("tm")
    ids = jnp.stack([lax.axis_index(a) for a in ("xh", "core", "tm")]).astype(jnp.int32)
    rows = traces.transpose(1, 0, 2)
    send = jnp.where(tm == 0, rows[2:], rows[:2])
    send, ids = lax.optimization_barrier((send, ids))
    peer = flip(send, "tm")
    mine, far, cross, fwd, env = call(
        first_kernel,
        (
            shape((2, 32, 128), jnp.int32),
            shape((2, 32, 128), jnp.int16),
            shape((2, 2, 32, 128), jnp.int16),
            shape((HALF, 2 * BAND), bf16),
            shape((HALF, 2 * FB), bf16),
        ),
        [SMEM, HBM],
        [
            pltpu.VMEM((32, 1024), jnp.int32),
            pltpu.VMEM((1024, 32), f32),
            pltpu.VMEM((2, 32, BAND + FB), f32),
            pltpu.SemaphoreType.DMA,
        ],
    )(ids, pltpu.with_memory_space_constraint(delays.T, pltpu.HBM))
    core_d = flip(cross, "core")
    inv = call(
        inverse_kernel, shape((HALF, 2 * BAND), bf16), [VMEM], [pltpu.VMEM((2, 32, BAND), f32)]
    )(mine)
    peer, core_d, inv = lax.optimization_barrier((peer, core_d, inv))
    e = call(front_kernel, shape((64, 2 * FB), bf16), [SMEM] + [VMEM] * 5)(ids, rows, peer, fwd, inv, env)
    far_d = flip(jnp.stack([far, core_d[1]]), "xh")
    core_e = flip(e, "core")
    far_e = flip(jnp.stack([e, core_e]), "xh")
    acc = call(
        near_kernel,
        shape((2, 512, 128), f32),
        [VMEM] * 4,
        [pltpu.VMEM((512, 128), f32), pltpu.VMEM((2, 512, 128), bf16)],
    )(mine, core_d, e, core_e)
    offsets, after = lax.optimization_barrier((offsets, acc[0, :8]))
    q = call(times_kernel, shape((2, 3, 2 * FB, TB), bf16), [SMEM, VMEM])(offsets, after)
    q, acc = lax.optimization_barrier((q, acc))
    part = call(
        far_kernel,
        shape((256, 512), bf16),
        [VMEM] * 3,
        [pltpu.VMEM((512, 128), f32), pltpu.VMEM((2, 512, 128), bf16), pltpu.VMEM((512, 128), f32)],
    )(far_d, far_e, acc)
    parts = lax.all_to_all(part.reshape(32, 8, 512), ("zh", "y", "xl"), 0, 0, tiled=True)
    return call(final_kernel, shape((2, 8, TB), f32), [VMEM] * 2)(parts.reshape(256, 512), q)


def solution(mesh):
    chan = ("xh", "xl", "zh", "y", "core")
    fine = Mesh(mesh.devices.reshape(2, 2, 4, 4, 2, 2), chan + ("tm",))
    placed = (P(chan, None, "tm"), P(None, chan), P("tm"))
    return jax.shard_map(
        on_device, mesh=fine, in_specs=placed, out_specs=P("tm", chan, None), check_vma=False
    )
```

```python
import math

import jax
import jax.numpy as jnp
from jax import lax
from jax.experimental import pallas as pl
from jax.experimental.pallas import tpu as pltpu
from jax.sharding import Mesh
from jax.sharding import PartitionSpec as P

SAMPLES = 2048
HALF = 1024
BAND = 512
FB = 128
TB = 256
BAND_LO = 128
DEC = 8
CHANNELS = 4096
epsilon = 1e-06
bf16 = jnp.bfloat16
f32 = jnp.float32
VMEM = pl.BlockSpec(memory_space=pltpu.VMEM)
SMEM = pl.BlockSpec(memory_space=pltpu.SMEM)
HBM = pl.BlockSpec(memory_space=pltpu.HBM)


def half_turn(u):
    v = u * u
    s = 1.0 + v * (-1 / 6 + v * (1 / 120 + v * (-1 / 5040 + v * (1 / 362880 + v * (-1 / 39916800)))))
    c = 1.0 + v * (
        -1 / 2 + v * (1 / 24 + v * (-1 / 720 + v * (1 / 40320 + v * (-1 / 3628800 + v * (1 / 479001600)))))
    )
    return -(u * s), c


def circle(p):
    c, s = half_turn(((p & (SAMPLES - 1)) - HALF).astype(f32) * (math.pi / SAMPLES))
    return c * c - s * s, 2.0 * c * s


def iota(dims, axis):
    return lax.broadcasted_iota(jnp.int32, dims, axis)


def turn(u, v):
    return u[0] * v[0] - u[1] * v[1], u[0] * v[1] + u[1] * v[0]


def each_block(freq, base, store):
    step = iota(freq.shape, 0) * freq
    base[0], base[1] = circle(32 * step)
    low = circle(step)

    def body(a, _):
        at = pl.ds(pl.multiple_of(32 * a, 32), 32)
        store(at, *turn((base[0, pl.ds(a, 1), :], base[1, pl.ds(a, 1), :]), low))
        return 0

    lax.fori_loop(0, 32, body, 0, unroll=2)


def band(lane):
    return BAND_LO + 2 * (lane & (BAND // 2 - 1)) + (lane >> 8)


def store_band(ref, at, c, s):
    h = BAND // 2
    for i in range(2):
        ref[at, 2 * h * i : 2 * h * i + h] = c[:, h * i : h * i + h].astype(bf16)
        ref[at, 2 * h * i + h : 2 * h * i + 2 * h] = s[:, h * i : h * i + h].astype(bf16)


def first_kernel(ids, d_hbm, mine, cross, far, fwd_ref, env_ref, d_ref, rows, base, sem):
    copy = pltpu.make_async_copy(d_hbm, d_ref, sem)
    copy.start()
    lane = iota((32, BAND + FB), 1)

    def store(at, c, s):
        store_band(fwd_ref, at, c[:, :BAND], -s[:, :BAND])
        env_ref[at, :FB] = c[:, BAND:].astype(bf16)
        env_ref[at, FB:] = (-s[:, BAND:]).astype(bf16)

    each_block(jnp.where(lane < BAND, band(lane & (BAND - 1)), lane - BAND + 1), base, store)
    copy.wait()
    xh, core = ids[0], ids[1]
    for m in range(8):
        rows[pl.ds(128 * m, 128), :] = d_ref[:, pl.ds(128 * m, 128)].astype(f32).T

    def nodes(h, b, j):
        parts = []
        for zh in (2 * j, 2 * j + 1):
            for y in range(4):
                for xl in range(2):
                    x = 2 * (xh ^ h) + xl
                    at = pl.multiple_of((((x * 4 + zh) * 4 + y) * 2 + (core ^ b)) * 8, 8)
                    parts.append(rows[pl.ds(at, 8), :])
        return jnp.concatenate(parts, axis=0).T.astype(jnp.int32)

    for j in range(2):
        mine[j] = nodes(0, 0, j)
        d, lanes = nodes(0, 1, j), pl.ds(128 * j, 128)
        cross[0:32, lanes] = (d >> 3).astype(f32).astype(bf16)
        cross[32:64, lanes] = (d & 7).astype(f32).astype(bf16)
        for b in range(2):
            far[b, j] = nodes(1, b, j).astype(jnp.int16)


def split(v):
    high = v.astype(bf16).astype(f32)
    middle = (v - high).astype(bf16).astype(f32)
    return high, middle, (v - high) - middle


def times_kernel(offs, after, q_ref):
    scale = 1.0 / math.sqrt(FB * CHANNELS)
    for w in range(2):
        c, s = circle((1 + iota((FB, TB), 0)) * (DEC * iota((FB, TB), 1) + offs[w]))
        for i, (re, im) in enumerate(zip(split(c * scale), split(s * -scale))):
            q_ref[w, i, :FB] = re.astype(bf16)
            q_ref[w, i, FB:] = im.astype(bf16)


def inverse_kernel(after, inv_ref, base):
    _, taper = circle(2 * (band(iota((1, BAND), 1)) - BAND_LO) + 1)
    weight = taper * taper * (2.0 / SAMPLES)

    def store(at, c, s):
        store_band(inv_ref, at, weight * c, weight * s)

    each_block(band(iota((32, BAND), 1)), base, store)


def front_kernel(ids, own_ref, peer_ref, fwd_ref, inv_ref, env_ref, cross, message):
    tm = ids[2]
    own = own_ref[pl.ds(2 * tm, 2)].reshape(64, HALF)
    peer = peer_ref[...].reshape(64, HALF)
    terms = jnp.dot(jnp.concatenate([own, peer], axis=0), fwd_ref[...], preferred_element_type=f32)
    even = terms[:64, :BAND] + terms[64:, :BAND]
    odd = (terms[:64, BAND:] - terms[64:, BAND:]) * jnp.where(tm == 0, 1.0, -1.0)
    halves = []
    for i, v in enumerate((even, odd)):
        re, im = v[:, : BAND // 2], v[:, BAND // 2 :]
        forms = jnp.concatenate(
            [jnp.concatenate([re, -im], axis=1), jnp.concatenate([im, re], axis=1)], axis=0
        ).astype(bf16)
        table = inv_ref[:, BAND * i : BAND * (i + 1)]
        halves.append(lax.dot_general(forms, table, (((1,), (1,)), ((), ())), preferred_element_type=f32))
    first, second = halves[0] + halves[1], halves[0] - halves[1]
    energy = jnp.concatenate([v[:64] * v[:64] + v[64:] * v[64:] for v in (first, second)], axis=0)
    sums = jnp.sum(energy, axis=1, keepdims=True)
    sums = sums[:64] + sums[64:]
    env = jnp.dot(energy.astype(bf16), env_ref[...], preferred_element_type=f32)
    lane = lax.broadcasted_iota(jnp.int32, (1, 2 * FB), 1)
    flip_sign = (2 * (lane & 1) - 1).astype(f32)
    env = env[:64] + env[64:] * flip_sign
    factor = 1.0 / (math.sqrt(SAMPLES) * (sums / SAMPLES + epsilon))
    message[0:64] = (env * factor).astype(bf16)
    message[64:128] = cross[...]


def expand(normal, lhs):
    normal = normal.astype(f32)
    kept = (iota((FB, 128), 0) & 1) == (iota((FB, 128), 1) >> 6)
    for w in range(2):
        re = normal[32 * w : 32 * w + 32, :FB]
        im = normal[32 * w : 32 * w + 32, FB:]
        for part, quad in enumerate(((re, -im, re, -im), (im, re, im, re))):
            t = jnp.concatenate(quad, axis=0).T
            lhs[pl.ds(2 * w + part, FB, stride=4), :] = jnp.where(kept, t, 0.0)


def whole(d):
    return d if d.dtype == f32 else d.astype(jnp.int32).astype(f32)


def stack(delays, lhs, store):
    one = [half_turn((whole(d) - 512.0) * (math.pi / 1024)) for d in delays]
    two = [turn(v, v) for v in one]
    mid = two
    for i in range(FB // 4):
        powers, ahead = [[], [], [], []], []
        for (c, s), (c1, s1), v2 in zip(mid, one, two):
            cc, ss, cs, sc = c * c1, s * s1, c * s1, s * c1
            last = turn((c, s), v2)
            for group, v in zip(powers, ((cc + ss, sc - cs), (c, s), (cc - ss, sc + cs), last)):
                group.append([x.astype(bf16) for x in v])
            ahead.append(turn(last, v2))
        mid = ahead
        at = 16 * i
        a = jnp.concatenate([v[at : at + 16, :] for v in lhs], axis=1)
        for g in range(2):
            z = [x for even, odd in zip(powers[2 * g], powers[2 * g + 1]) for x in (*even, *odd)]
            r = jnp.dot(a, jnp.concatenate(z, axis=0), preferred_element_type=f32)
            store(at + 8 * g, r[8 * g : 8 * g + 8])


def near_kernel(own_d, message, core_message, acc_ref, wide, lhs):
    for i, e in enumerate((message, core_message)):
        expand(e[0:64], wide)
        lhs[i] = wide[...].astype(bf16)
    for j in range(2):
        lanes = slice(128 * j, 128 * j + 128)
        core_d = core_message[64:96, lanes].astype(f32) * 8.0 + core_message[96:128, lanes].astype(f32)

        def store(at, r):
            acc_ref[j, at : at + 8, :] = r

        stack((own_d[j], core_d), (lhs.at[0], lhs.at[1]), store)


def far_kernel(far_d, diag_d, far_e, acc_ref, out_ref, wide, lhs, acc):
    for i in range(2):
        expand(far_e[i], wide)
        lhs[i] = wide[...].astype(bf16)
    for j in range(2):

        def store(at, r):
            acc[at : at + 8, :] = acc_ref[j, at : at + 8, :] + r

        stack((far_d[0, j], diag_d[1, j]), (lhs.at[0], lhs.at[1]), store)
        for q in range(4):
            out_ref[128 * j : 128 * j + 128, 128 * q : 128 * q + 128] = acc[pl.ds(q, FB, stride=4), :].T.astype(bf16)


def final_kernel(part_ref, q_ref, out_ref):
    total = part_ref[0:16, :].astype(f32)
    for i in range(1, 16):
        total = total + part_ref[16 * i : 16 * i + 16, :].astype(f32)
    total = total[:8] + total[8:]
    zero = jnp.zeros((8, TB), f32)
    for w in range(2):
        a = jnp.concatenate([*split(total[:, w * TB : (w + 1) * TB]), zero], axis=0).astype(bf16)
        r = [jnp.dot(a, q_ref[w, i], preferred_element_type=f32) for i in range(3)]
        out_ref[w] = (r[0][:8] + ((r[0][8:16] + r[1][:8]) + ((r[0][16:24] + r[1][8:16]) + r[2][:8])))


def call(kernel, outs, ins, scratch=(), limit=24):
    return pl.pallas_call(
        kernel,
        out_shape=outs,
        in_specs=ins,
        out_specs=jax.tree.map(lambda _: VMEM, outs),
        scratch_shapes=list(scratch),
        compiler_params=pltpu.CompilerParams(vmem_limit_bytes=limit << 20),
    )


def flip(v, *axes):
    n = 2 ** len(axes)
    return lax.ppermute(v, axes, [(i, n - 1 - i) for i in range(n)])


def shape(dims, dtype):
    return jax.ShapeDtypeStruct(dims, dtype)


def on_device(traces, delays, offsets):
    tm = lax.axis_index("tm")
    ids = jnp.stack([lax.axis_index(a) for a in ("xh", "core", "tm")]).astype(jnp.int32)
    rows = traces.transpose(1, 0, 2)
    send = jnp.where(tm == 0, rows[2:], rows[:2])
    send, ids = lax.optimization_barrier((send, ids))
    peer = flip(send, "tm")
    mine, cross, far, fwd, env = call(
        first_kernel,
        (
            shape((2, 32, 128), jnp.int32),
            shape((64, 256), bf16),
            shape((2, 2, 32, 128), jnp.int16),
            shape((HALF, 2 * BAND), bf16),
            shape((HALF, 2 * FB), bf16),
        ),
        [SMEM, HBM],
        [
            pltpu.VMEM((32, 1024), jnp.int32),
            pltpu.VMEM((1024, 32), f32),
            pltpu.VMEM((2, 32, BAND + FB), f32),
            pltpu.SemaphoreType.DMA,
        ],
    )(ids, pltpu.with_memory_space_constraint(delays.T, pltpu.HBM))
    far_d = flip(far, "xh")
    inv = call(
        inverse_kernel, shape((HALF, 2 * BAND), bf16), [VMEM], [pltpu.VMEM((2, 32, BAND), f32)]
    )(mine)
    peer, far, inv = lax.optimization_barrier((peer, far, inv))
    message = call(front_kernel, shape((128, 2 * FB), bf16), [SMEM] + [VMEM] * 6)(
        ids, rows, peer, fwd, inv, env, cross
    )
    core_message = flip(message, "core")
    far_e = flip(jnp.stack([message[:64], core_message[:64]]), "xh")
    acc = call(
        near_kernel,
        shape((2, 512, 128), f32),
        [VMEM] * 3,
        [pltpu.VMEM((512, 128), f32), pltpu.VMEM((2, 512, 128), bf16)],
    )(mine, message, core_message)
    far_d, acc = lax.optimization_barrier((far_d, acc))
    diag_d = flip(far_d, "core")
    offsets, after = lax.optimization_barrier((offsets, acc[0, :8]))
    q = call(times_kernel, shape((2, 3, 2 * FB, TB), bf16), [SMEM, VMEM])(offsets, after)
    q, acc = lax.optimization_barrier((q, acc))
    part = call(
        far_kernel,
        shape((256, 512), bf16),
        [VMEM] * 4,
        [pltpu.VMEM((512, 128), f32), pltpu.VMEM((2, 512, 128), bf16), pltpu.VMEM((512, 128), f32)],
    )(far_d, diag_d, far_e, acc)
    parts = lax.all_to_all(part.reshape(32, 8, 512), ("zh", "y", "xl"), 0, 0, tiled=True)
    return call(final_kernel, shape((2, 8, TB), f32), [VMEM] * 2)(parts.reshape(256, 512), q)


def solution(mesh):
    chan = ("xh", "xl", "zh", "y", "core")
    fine = Mesh(mesh.devices.reshape(2, 2, 4, 4, 2, 2), chan + ("tm",))
    placed = (P(chan, None, "tm"), P(None, chan), P("tm"))
    return jax.shard_map(
        on_device, mesh=fine, in_specs=placed, out_specs=P("tm", chan, None), check_vma=False
    )
```

```python
import math

import jax
import jax.numpy as jnp
from jax import lax
from jax.experimental import pallas as pl
from jax.experimental.pallas import tpu as pltpu
from jax.sharding import Mesh
from jax.sharding import PartitionSpec as P

SAMPLES = 2048
HALF = 1024
BAND = 512
FB = 128
TB = 256
BAND_LO = 128
DEC = 8
CHANNELS = 4096
epsilon = 1e-06
bf16 = jnp.bfloat16
f32 = jnp.float32
VMEM = pl.BlockSpec(memory_space=pltpu.VMEM)
SMEM = pl.BlockSpec(memory_space=pltpu.SMEM)
HBM = pl.BlockSpec(memory_space=pltpu.HBM)


def half_turn(u):
    v = u * u
    s = 1.0 + v * (-1 / 6 + v * (1 / 120 + v * (-1 / 5040 + v * (1 / 362880 + v * (-1 / 39916800)))))
    c = 1.0 + v * (
        -1 / 2 + v * (1 / 24 + v * (-1 / 720 + v * (1 / 40320 + v * (-1 / 3628800 + v * (1 / 479001600)))))
    )
    return -(u * s), c


def circle(p):
    c, s = half_turn(((p & (SAMPLES - 1)) - HALF).astype(f32) * (math.pi / SAMPLES))
    return c * c - s * s, 2.0 * c * s


def iota(dims, axis):
    return lax.broadcasted_iota(jnp.int32, dims, axis)


def turn(u, v):
    return u[0] * v[0] - u[1] * v[1], u[0] * v[1] + u[1] * v[0]


def each_block(freq, base, store):
    step = iota(freq.shape, 0) * freq
    base[0], base[1] = circle(32 * step)
    low = circle(step)

    def body(a, _):
        at = pl.ds(pl.multiple_of(32 * a, 32), 32)
        store(at, *turn((base[0, pl.ds(a, 1), :], base[1, pl.ds(a, 1), :]), low))
        return 0

    lax.fori_loop(0, 32, body, 0, unroll=2)


def band(lane):
    return BAND_LO + 2 * (lane & (BAND // 2 - 1)) + (lane >> 8)


def store_band(ref, at, c, s):
    h = BAND // 2
    for i in range(2):
        ref[at, 2 * h * i : 2 * h * i + h] = c[:, h * i : h * i + h].astype(bf16)
        ref[at, 2 * h * i + h : 2 * h * i + 2 * h] = s[:, h * i : h * i + h].astype(bf16)


def first_kernel(ids, d_hbm, mine, far, cross, fwd_ref, env_ref, d_ref, rows, base, sem):
    copy = pltpu.make_async_copy(d_hbm, d_ref, sem)
    copy.start()
    lane = iota((32, BAND + FB), 1)

    def store(at, c, s):
        store_band(fwd_ref, at, c[:, :BAND], -s[:, :BAND])
        env_ref[at, :FB] = c[:, BAND:].astype(bf16)
        env_ref[at, FB:] = (-s[:, BAND:]).astype(bf16)

    each_block(jnp.where(lane < BAND, band(lane & (BAND - 1)), lane - BAND + 1), base, store)
    copy.wait()
    xh, core = ids[0], ids[1]
    for m in range(8):
        rows[pl.ds(128 * m, 128), :] = d_ref[:, pl.ds(128 * m, 128)].astype(f32).T

    def nodes(h, b, j):
        parts = []
        for zh in (2 * j, 2 * j + 1):
            for y in range(4):
                for xl in range(2):
                    x = 2 * (xh ^ h) + xl
                    at = pl.multiple_of((((x * 4 + zh) * 4 + y) * 2 + (core ^ b)) * 8, 8)
                    parts.append(rows[pl.ds(at, 8), :])
        return jnp.concatenate(parts, axis=0).T.astype(jnp.int32)

    for j in range(2):
        mine[j] = nodes(0, 0, j)
        far[j] = nodes(1, 0, j).astype(jnp.int16)
        for h in range(2):
            cross[h, j] = nodes(h, 1, j).astype(jnp.int16)


def split(v):
    high = v.astype(bf16).astype(f32)
    middle = (v - high).astype(bf16).astype(f32)
    return high, middle, (v - high) - middle


def times_kernel(offs, after, q_ref):
    scale = 1.0 / math.sqrt(FB * CHANNELS)
    for w in range(2):
        c, s = circle((1 + iota((FB, TB), 0)) * (DEC * iota((FB, TB), 1) + offs[w]))
        for i, (re, im) in enumerate(zip(split(c * scale), split(s * -scale))):
            q_ref[w, i, :FB] = re.astype(bf16)
            q_ref[w, i, FB:] = im.astype(bf16)


def inverse_kernel(after, inv_ref, base):
    _, taper = circle(2 * (band(iota((1, BAND), 1)) - BAND_LO) + 1)
    weight = taper * taper * (2.0 / SAMPLES)

    def store(at, c, s):
        store_band(inv_ref, at, weight * c, weight * s)

    each_block(band(iota((32, BAND), 1)), base, store)


def front_kernel(ids, own_ref, peer_ref, fwd_ref, inv_ref, env_ref, e_ref):
    tm = ids[2]
    own = own_ref[pl.ds(2 * tm, 2)].reshape(64, HALF)
    peer = peer_ref[...].reshape(64, HALF)
    terms = jnp.dot(jnp.concatenate([own, peer], axis=0), fwd_ref[...], preferred_element_type=f32)
    even = terms[:64, :BAND] + terms[64:, :BAND]
    odd = (terms[:64, BAND:] - terms[64:, BAND:]) * jnp.where(tm == 0, 1.0, -1.0)
    halves = []
    for i, v in enumerate((even, odd)):
        re, im = v[:, : BAND // 2], v[:, BAND // 2 :]
        forms = jnp.concatenate(
            [jnp.concatenate([re, -im], axis=1), jnp.concatenate([im, re], axis=1)], axis=0
        ).astype(bf16)
        table = inv_ref[:, BAND * i : BAND * (i + 1)]
        halves.append(lax.dot_general(forms, table, (((1,), (1,)), ((), ())), preferred_element_type=f32))
    first, second = halves[0] + halves[1], halves[0] - halves[1]
    energy = jnp.concatenate([v[:64] * v[:64] + v[64:] * v[64:] for v in (first, second)], axis=0)
    sums = jnp.sum(energy, axis=1, keepdims=True)
    sums = sums[:64] + sums[64:]
    env = jnp.dot(energy.astype(bf16), env_ref[...], preferred_element_type=f32)
    lane = lax.broadcasted_iota(jnp.int32, (1, 2 * FB), 1)
    flip_sign = (2 * (lane & 1) - 1).astype(f32)
    env = env[:64] + env[64:] * flip_sign
    factor = 1.0 / (math.sqrt(SAMPLES) * (sums / SAMPLES + epsilon))
    e_ref[...] = (env * factor).astype(bf16)


def expand(normal, lhs):
    normal = normal.astype(f32)
    kept = (iota((FB, 128), 0) & 1) == (iota((FB, 128), 1) >> 6)
    for w in range(2):
        re = normal[32 * w : 32 * w + 32, :FB]
        im = normal[32 * w : 32 * w + 32, FB:]
        for part, quad in enumerate(((re, -im, re, -im), (im, re, im, re))):
            t = jnp.concatenate(quad, axis=0).T
            lhs[pl.ds(2 * w + part, FB, stride=4), :] = jnp.where(kept, t, 0.0)


def stack(delays, lhs, store):
    one = [half_turn((d.astype(jnp.int32) - 512).astype(f32) * (math.pi / 1024)) for d in delays]
    two = [turn(v, v) for v in one]
    mid = two
    for i in range(FB // 4):
        powers, ahead = [[], [], [], []], []
        for (c, s), (c1, s1), v2 in zip(mid, one, two):
            cc, ss, cs, sc = c * c1, s * s1, c * s1, s * c1
            last = turn((c, s), v2)
            for group, v in zip(powers, ((cc + ss, sc - cs), (c, s), (cc - ss, sc + cs), last)):
                group.append([x.astype(bf16) for x in v])
            ahead.append(turn(last, v2))
        mid = ahead
        at = 16 * i
        a = jnp.concatenate([v[at : at + 16, :] for v in lhs], axis=1)
        for g in range(2):
            z = [x for even, odd in zip(powers[2 * g], powers[2 * g + 1]) for x in (*even, *odd)]
            r = jnp.dot(a, jnp.concatenate(z, axis=0), preferred_element_type=f32)
            store(at + 8 * g, r[8 * g : 8 * g + 8])


def near_kernel(own_d, core_d, own_e, core_e, acc_ref, wide, lhs):
    for i, e in enumerate((own_e, core_e)):
        expand(e[...], wide)
        lhs[i] = wide[...].astype(bf16)
    for j in range(2):

        def store(at, r):
            acc_ref[j, at : at + 8, :] = r

        stack((own_d[j], core_d[0, j]), (lhs.at[0], lhs.at[1]), store)


def far_kernel(far_d, far_e, acc_ref, out_ref, wide, lhs, acc):
    for i in range(2):
        expand(far_e[i], wide)
        lhs[i] = wide[...].astype(bf16)
    for j in range(2):

        def store(at, r):
            acc[at : at + 8, :] = acc_ref[j, at : at + 8, :] + r

        stack((far_d[0, j], far_d[1, j]), (lhs.at[0], lhs.at[1]), store)
        for q in range(4):
            out_ref[128 * j : 128 * j + 128, 128 * q : 128 * q + 128] = acc[pl.ds(q, FB, stride=4), :].T.astype(bf16)


def final_kernel(part_ref, q_ref, out_ref):
    total = part_ref[0:16, :].astype(f32)
    for i in range(1, 16):
        total = total + part_ref[16 * i : 16 * i + 16, :].astype(f32)
    total = total[:8] + total[8:]
    zero = jnp.zeros((8, TB), f32)
    for w in range(2):
        a = jnp.concatenate([*split(total[:, w * TB : (w + 1) * TB]), zero], axis=0).astype(bf16)
        r = [jnp.dot(a, q_ref[w, i], preferred_element_type=f32) for i in range(3)]
        out_ref[w] = (r[0][:8] + ((r[0][8:16] + r[1][:8]) + ((r[0][16:24] + r[1][8:16]) + r[2][:8])))


def call(kernel, outs, ins, scratch=(), limit=24):
    return pl.pallas_call(
        kernel,
        out_shape=outs,
        in_specs=ins,
        out_specs=jax.tree.map(lambda _: VMEM, outs),
        scratch_shapes=list(scratch),
        compiler_params=pltpu.CompilerParams(vmem_limit_bytes=limit << 20),
    )


def flip(v, *axes):
    n = 2 ** len(axes)
    return lax.ppermute(v, axes, [(i, n - 1 - i) for i in range(n)])


def shape(dims, dtype):
    return jax.ShapeDtypeStruct(dims, dtype)


def on_device(traces, delays, offsets):
    tm = lax.axis_index("tm")
    ids = jnp.stack([lax.axis_index(a) for a in ("xh", "core", "tm")]).astype(jnp.int32)
    rows = traces.transpose(1, 0, 2)
    send = jnp.where(tm == 0, rows[2:], rows[:2])
    send, ids = lax.optimization_barrier((send, ids))
    peer = flip(send, "tm")
    mine, far, cross, fwd, env = call(
        first_kernel,
        (
            shape((2, 32, 128), jnp.int32),
            shape((2, 32, 128), jnp.int16),
            shape((2, 2, 32, 128), jnp.int16),
            shape((HALF, 2 * BAND), bf16),
            shape((HALF, 2 * FB), bf16),
        ),
        [SMEM, HBM],
        [
            pltpu.VMEM((32, 1024), jnp.int32),
            pltpu.VMEM((1024, 32), f32),
            pltpu.VMEM((2, 32, BAND + FB), f32),
            pltpu.SemaphoreType.DMA,
        ],
    )(ids, pltpu.with_memory_space_constraint(delays.T, pltpu.HBM))
    core_d = flip(cross, "core")
    inv = call(
        inverse_kernel, shape((HALF, 2 * BAND), bf16), [VMEM], [pltpu.VMEM((2, 32, BAND), f32)]
    )(mine)
    peer, core_d, inv = lax.optimization_barrier((peer, core_d, inv))
    e = call(front_kernel, shape((64, 2 * FB), bf16), [SMEM] + [VMEM] * 5)(ids, rows, peer, fwd, inv, env)
    far_d = flip(jnp.stack([far, core_d[1]]), "xh", "xl")
    core_e = flip(e, "core")
    far_e = flip(jnp.stack([e, core_e]), "xh", "xl")
    acc = call(
        near_kernel,
        shape((2, 512, 128), f32),
        [VMEM] * 4,
        [pltpu.VMEM((512, 128), f32), pltpu.VMEM((2, 512, 128), bf16)],
    )(mine, core_d, e, core_e)
    offsets, after = lax.optimization_barrier((offsets, acc[0, :8]))
    q = call(times_kernel, shape((2, 3, 2 * FB, TB), bf16), [SMEM, VMEM])(offsets, after)
    q, acc = lax.optimization_barrier((q, acc))
    part = call(
        far_kernel,
        shape((256, 512), bf16),
        [VMEM] * 3,
        [pltpu.VMEM((512, 128), f32), pltpu.VMEM((2, 512, 128), bf16), pltpu.VMEM((512, 128), f32)],
    )(far_d, far_e, acc)
    parts = lax.all_to_all(part.reshape(32, 8, 512), ("zh", "y", "xl"), 0, 0, tiled=True)
    return call(final_kernel, shape((2, 8, TB), f32), [VMEM] * 2)(parts.reshape(256, 512), q)


def solution(mesh):
    chan = ("xh", "xl", "zh", "y", "core")
    fine = Mesh(mesh.devices.reshape(2, 2, 4, 4, 2, 2), chan + ("tm",))
    placed = (P(chan, None, "tm"), P(None, chan), P("tm"))
    return jax.shard_map(
        on_device, mesh=fine, in_specs=placed, out_specs=P("tm", chan, None), check_vma=False
    )
```

```python
import math

import jax
import jax.numpy as jnp
from jax import lax
from jax.experimental import pallas as pl
from jax.experimental.pallas import tpu as pltpu
from jax.sharding import Mesh
from jax.sharding import PartitionSpec as P

SAMPLES = 2048
HALF = 1024
BAND = 512
FB = 128
TB = 256
BAND_LO = 128
DEC = 8
CHANNELS = 4096
epsilon = 1e-06
bf16 = jnp.bfloat16
f32 = jnp.float32
VMEM = pl.BlockSpec(memory_space=pltpu.VMEM)
SMEM = pl.BlockSpec(memory_space=pltpu.SMEM)
HBM = pl.BlockSpec(memory_space=pltpu.HBM)


def half_turn(u):
    v = u * u
    s = 1.0 + v * (-1 / 6 + v * (1 / 120 + v * (-1 / 5040 + v * (1 / 362880 + v * (-1 / 39916800)))))
    c = 1.0 + v * (
        -1 / 2 + v * (1 / 24 + v * (-1 / 720 + v * (1 / 40320 + v * (-1 / 3628800 + v * (1 / 479001600)))))
    )
    return -(u * s), c


def circle(p):
    c, s = half_turn(((p & (SAMPLES - 1)) - HALF).astype(f32) * (math.pi / SAMPLES))
    return c * c - s * s, 2.0 * c * s


def iota(dims, axis):
    return lax.broadcasted_iota(jnp.int32, dims, axis)


def turn(u, v):
    return u[0] * v[0] - u[1] * v[1], u[0] * v[1] + u[1] * v[0]


def each_block(freq, base, store):
    step = iota(freq.shape, 0) * freq
    base[0], base[1] = circle(32 * step)
    low = circle(step)

    def body(a, _):
        at = pl.ds(pl.multiple_of(32 * a, 32), 32)
        store(at, *turn((base[0, pl.ds(a, 1), :], base[1, pl.ds(a, 1), :]), low))
        return 0

    lax.fori_loop(0, 32, body, 0, unroll=2)


def band(lane):
    return BAND_LO + 2 * (lane & (BAND // 2 - 1)) + (lane >> 8)


def store_band(ref, at, c, s):
    h = BAND // 2
    for i in range(2):
        ref[at, 2 * h * i : 2 * h * i + h] = c[:, h * i : h * i + h].astype(bf16)
        ref[at, 2 * h * i + h : 2 * h * i + 2 * h] = s[:, h * i : h * i + h].astype(bf16)


def first_kernel(ids, d_hbm, mine, far, cross, fwd_ref, env_ref, d_ref, rows, base, sem):
    copy = pltpu.make_async_copy(d_hbm, d_ref, sem)
    copy.start()
    lane = iota((32, BAND + FB), 1)

    def store(at, c, s):
        store_band(fwd_ref, at, c[:, :BAND], -s[:, :BAND])
        env_ref[at, :FB] = c[:, BAND:].astype(bf16)
        env_ref[at, FB:] = (-s[:, BAND:]).astype(bf16)

    each_block(jnp.where(lane < BAND, band(lane & (BAND - 1)), lane - BAND + 1), base, store)
    copy.wait()
    xh, core = ids[0], ids[1]
    for m in range(8):
        rows[pl.ds(128 * m, 128), :] = d_ref[:, pl.ds(128 * m, 128)].astype(f32).T

    def nodes(h, b, j):
        parts = []
        for zh in (2 * j, 2 * j + 1):
            for y in range(4):
                for xl in range(2):
                    x = 2 * (xh ^ h) + xl
                    at = pl.multiple_of((((x * 4 + zh) * 4 + y) * 2 + (core ^ b)) * 8, 8)
                    parts.append(rows[pl.ds(at, 8), :])
        return jnp.concatenate(parts, axis=0).T.astype(jnp.int32)

    for j in range(2):
        mine[j] = nodes(0, 0, j)
        far[j] = nodes(1, 0, j).astype(jnp.int16)
        for h in range(2):
            cross[h, j] = nodes(h, 1, j).astype(jnp.int16)


def split(v):
    high = v.astype(bf16).astype(f32)
    middle = (v - high).astype(bf16).astype(f32)
    return high, middle, (v - high) - middle


def times_kernel(offs, after, q_ref):
    scale = 1.0 / math.sqrt(FB * CHANNELS)
    for w in range(2):
        at = DEC * iota((16, TB), 1) + offs[w]
        low = circle((1 + iota((16, TB), 0)) * at)
        high = circle(16 * iota((16, TB), 0) * at)
        for a in range(FB // 16):
            c, s = turn([v[a : a + 1] for v in high], low)
            for i, (re, im) in enumerate(zip(split(c * scale), split(s * -scale))):
                q_ref[w, i, 16 * a : 16 * a + 16] = re.astype(bf16)
                q_ref[w, i, FB + 16 * a : FB + 16 * a + 16] = im.astype(bf16)


def inverse_kernel(after, inv_ref, base):
    _, taper = circle(2 * (band(iota((1, BAND), 1)) - BAND_LO) + 1)
    weight = taper * taper * (2.0 / SAMPLES)

    def store(at, c, s):
        store_band(inv_ref, at, weight * c, weight * s)

    each_block(band(iota((32, BAND), 1)), base, store)


def front_kernel(ids, own_ref, peer_ref, fwd_ref, inv_ref, env_ref, e_ref):
    tm = ids[2]
    own = own_ref[pl.ds(2 * tm, 2)].reshape(64, HALF)
    peer = peer_ref[...].reshape(64, HALF)
    terms = jnp.dot(jnp.concatenate([own, peer], axis=0), fwd_ref[...], preferred_element_type=f32)
    even = terms[:64, :BAND] + terms[64:, :BAND]
    odd = (terms[:64, BAND:] - terms[64:, BAND:]) * jnp.where(tm == 0, 1.0, -1.0)
    halves = []
    for i, v in enumerate((even, odd)):
        re, im = v[:, : BAND // 2], v[:, BAND // 2 :]
        forms = jnp.concatenate(
            [jnp.concatenate([re, -im], axis=1), jnp.concatenate([im, re], axis=1)], axis=0
        ).astype(bf16)
        table = inv_ref[:, BAND * i : BAND * (i + 1)]
        halves.append(lax.dot_general(forms, table, (((1,), (1,)), ((), ())), preferred_element_type=f32))
    first, second = halves[0] + halves[1], halves[0] - halves[1]
    energy = jnp.concatenate([v[:64] * v[:64] + v[64:] * v[64:] for v in (first, second)], axis=0)
    sums = jnp.sum(energy, axis=1, keepdims=True)
    sums = sums[:64] + sums[64:]
    env = jnp.dot(energy.astype(bf16), env_ref[...], preferred_element_type=f32)
    lane = lax.broadcasted_iota(jnp.int32, (1, 2 * FB), 1)
    flip_sign = (2 * (lane & 1) - 1).astype(f32)
    env = env[:64] + env[64:] * flip_sign
    factor = 1.0 / (math.sqrt(SAMPLES) * (sums / SAMPLES + epsilon))
    e_ref[...] = (env * factor).astype(bf16)


def expand(normal, lhs):
    normal = normal.astype(f32)
    kept = (iota((FB, 128), 0) & 1) == (iota((FB, 128), 1) >> 6)
    for w in range(2):
        re = normal[32 * w : 32 * w + 32, :FB]
        im = normal[32 * w : 32 * w + 32, FB:]
        for part, quad in enumerate(((re, -im, re, -im), (im, re, im, re))):
            t = jnp.concatenate(quad, axis=0).T
            lhs[pl.ds(2 * w + part, FB, stride=4), :] = jnp.where(kept, t, 0.0)


def stack(delays, lhs, store):
    one = [half_turn((d.astype(jnp.int32) - 512).astype(f32) * (math.pi / 1024)) for d in delays]
    two = [turn(v, v) for v in one]
    mid = two
    for i in range(FB // 4):
        powers, ahead = [[], [], [], []], []
        for (c, s), (c1, s1), v2 in zip(mid, one, two):
            cc, ss, cs, sc = c * c1, s * s1, c * s1, s * c1
            last = turn((c, s), v2)
            for group, v in zip(powers, ((cc + ss, sc - cs), (c, s), (cc - ss, sc + cs), last)):
                group.append([x.astype(bf16) for x in v])
            ahead.append(turn(last, v2))
        mid = ahead
        at = 16 * i
        a = jnp.concatenate([v[at : at + 16, :] for v in lhs], axis=1)
        for g in range(2):
            z = [x for even, odd in zip(powers[2 * g], powers[2 * g + 1]) for x in (*even, *odd)]
            r = jnp.dot(a, jnp.concatenate(z, axis=0), preferred_element_type=f32)
            store(at + 8 * g, r[8 * g : 8 * g + 8])


def near_kernel(own_d, core_d, own_e, core_e, acc_ref, wide, lhs):
    for i, e in enumerate((own_e, core_e)):
        expand(e[...], wide)
        lhs[i] = wide[...].astype(bf16)
    for j in range(2):

        def store(at, r):
            acc_ref[j, at : at + 8, :] = r

        stack((own_d[j], core_d[0, j]), (lhs.at[0], lhs.at[1]), store)


def far_kernel(far_d, far_e, acc_ref, out_ref, wide, lhs, acc):
    for i in range(2):
        expand(far_e[i], wide)
        lhs[i] = wide[...].astype(bf16)
    for j in range(2):

        def store(at, r):
            acc[at : at + 8, :] = acc_ref[j, at : at + 8, :] + r

        stack((far_d[0, j], far_d[1, j]), (lhs.at[0], lhs.at[1]), store)
        for q in range(4):
            out_ref[128 * j : 128 * j + 128, 128 * q : 128 * q + 128] = acc[pl.ds(q, FB, stride=4), :].T.astype(bf16)


def final_kernel(part_ref, q_ref, out_ref):
    total = part_ref[0:16, :].astype(f32)
    for i in range(1, 16):
        total = total + part_ref[16 * i : 16 * i + 16, :].astype(f32)
    total = total[:8] + total[8:]
    zero = jnp.zeros((8, TB), f32)
    for w in range(2):
        a = jnp.concatenate([*split(total[:, w * TB : (w + 1) * TB]), zero], axis=0).astype(bf16)
        r = [jnp.dot(a, q_ref[w, i], preferred_element_type=f32) for i in range(3)]
        out_ref[w] = (r[0][:8] + ((r[0][8:16] + r[1][:8]) + ((r[0][16:24] + r[1][8:16]) + r[2][:8])))


def call(kernel, outs, ins, scratch=(), limit=24):
    return pl.pallas_call(
        kernel,
        out_shape=outs,
        in_specs=ins,
        out_specs=jax.tree.map(lambda _: VMEM, outs),
        scratch_shapes=list(scratch),
        compiler_params=pltpu.CompilerParams(vmem_limit_bytes=limit << 20),
    )


def flip(v, *axes):
    n = 2 ** len(axes)
    return lax.ppermute(v, axes, [(i, n - 1 - i) for i in range(n)])


def shape(dims, dtype):
    return jax.ShapeDtypeStruct(dims, dtype)


def on_device(traces, delays, offsets):
    tm = lax.axis_index("tm")
    ids = jnp.stack([lax.axis_index(a) for a in ("xh", "core", "tm")]).astype(jnp.int32)
    rows = traces.transpose(1, 0, 2)
    send = jnp.where(tm == 0, rows[2:], rows[:2])
    send, ids = lax.optimization_barrier((send, ids))
    peer = flip(send, "tm")
    mine, far, cross, fwd, env = call(
        first_kernel,
        (
            shape((2, 32, 128), jnp.int32),
            shape((2, 32, 128), jnp.int16),
            shape((2, 2, 32, 128), jnp.int16),
            shape((HALF, 2 * BAND), bf16),
            shape((HALF, 2 * FB), bf16),
        ),
        [SMEM, HBM],
        [
            pltpu.VMEM((32, 1024), jnp.int32),
            pltpu.VMEM((1024, 32), f32),
            pltpu.VMEM((2, 32, BAND + FB), f32),
            pltpu.SemaphoreType.DMA,
        ],
    )(ids, pltpu.with_memory_space_constraint(delays.T, pltpu.HBM))
    core_d = flip(cross, "core")
    inv = call(
        inverse_kernel, shape((HALF, 2 * BAND), bf16), [VMEM], [pltpu.VMEM((2, 32, BAND), f32)]
    )(mine)
    peer, core_d, inv = lax.optimization_barrier((peer, core_d, inv))
    e = call(front_kernel, shape((64, 2 * FB), bf16), [SMEM] + [VMEM] * 5)(ids, rows, peer, fwd, inv, env)
    far_d = flip(jnp.stack([far, core_d[1]]), "xh", "xl")
    core_e = flip(e, "core")
    far_e = flip(jnp.stack([e, core_e]), "xh", "xl")
    acc = call(
        near_kernel,
        shape((2, 512, 128), f32),
        [VMEM] * 4,
        [pltpu.VMEM((512, 128), f32), pltpu.VMEM((2, 512, 128), bf16)],
    )(mine, core_d, e, core_e)
    offsets, after = lax.optimization_barrier((offsets, acc[0, :8]))
    q = call(times_kernel, shape((2, 3, 2 * FB, TB), bf16), [SMEM, VMEM])(offsets, after)
    q, acc = lax.optimization_barrier((q, acc))
    part = call(
        far_kernel,
        shape((256, 512), bf16),
        [VMEM] * 3,
        [pltpu.VMEM((512, 128), f32), pltpu.VMEM((2, 512, 128), bf16), pltpu.VMEM((512, 128), f32)],
    )(far_d, far_e, acc)
    parts = lax.all_to_all(part.reshape(32, 8, 512), ("zh", "y", "xl"), 0, 0, tiled=True)
    return call(final_kernel, shape((2, 8, TB), f32), [VMEM] * 2)(parts.reshape(256, 512), q)


def solution(mesh):
    chan = ("xh", "xl", "zh", "y", "core")
    fine = Mesh(mesh.devices.reshape(2, 2, 4, 4, 2, 2), chan + ("tm",))
    placed = (P(chan, None, "tm"), P(None, chan), P("tm"))
    return jax.shard_map(
        on_device, mesh=fine, in_specs=placed, out_specs=P("tm", chan, None), check_vma=False
    )
```

```python
import math

import jax
import jax.numpy as jnp
from jax import lax
from jax.experimental import pallas as pl
from jax.experimental.pallas import tpu as pltpu
from jax.sharding import Mesh
from jax.sharding import PartitionSpec as P

SAMPLES = 2048
HALF = 1024
BAND = 512
FB = 128
TB = 256
BAND_LO = 128
DEC = 8
CHANNELS = 4096
epsilon = 1e-06
bf16 = jnp.bfloat16
f32 = jnp.float32
VMEM = pl.BlockSpec(memory_space=pltpu.VMEM)
SMEM = pl.BlockSpec(memory_space=pltpu.SMEM)
HBM = pl.BlockSpec(memory_space=pltpu.HBM)


def half_turn(u):
    v = u * u
    s = 1.0 + v * (-1 / 6 + v * (1 / 120 + v * (-1 / 5040 + v * (1 / 362880 + v * (-1 / 39916800)))))
    c = 1.0 + v * (
        -1 / 2 + v * (1 / 24 + v * (-1 / 720 + v * (1 / 40320 + v * (-1 / 3628800 + v * (1 / 479001600)))))
    )
    return -(u * s), c


def circle(p):
    c, s = half_turn(((p & (SAMPLES - 1)) - HALF).astype(f32) * (math.pi / SAMPLES))
    return c * c - s * s, 2.0 * c * s


def iota(dims, axis):
    return lax.broadcasted_iota(jnp.int32, dims, axis)


def turn(u, v):
    return u[0] * v[0] - u[1] * v[1], u[0] * v[1] + u[1] * v[0]


def each_block(freq, base, store):
    step = iota(freq.shape, 0) * freq
    base[0], base[1] = circle(32 * step)
    low = circle(step)

    def body(a, _):
        at = pl.ds(pl.multiple_of(32 * a, 32), 32)
        store(at, *turn((base[0, pl.ds(a, 1), :], base[1, pl.ds(a, 1), :]), low))
        return 0

    lax.fori_loop(0, 32, body, 0, unroll=2)


def band(lane):
    return BAND_LO + 2 * (lane & (BAND // 2 - 1)) + (lane >> 8)


def store_band(ref, at, c, s):
    h = BAND // 2
    for i in range(2):
        ref[at, 2 * h * i : 2 * h * i + h] = c[:, h * i : h * i + h].astype(bf16)
        ref[at, 2 * h * i + h : 2 * h * i + 2 * h] = s[:, h * i : h * i + h].astype(bf16)


def first_kernel(ids, d_hbm, after, mine, far, cross, fwd_ref, env_ref, d_ref, rows, base, sem):
    copy = pltpu.make_async_copy(d_hbm, d_ref, sem)
    copy.start()
    lane = iota((32, BAND + FB), 1)

    def store(at, c, s):
        store_band(fwd_ref, at, c[:, :BAND], -s[:, :BAND])
        env_ref[at, :FB] = c[:, BAND:].astype(bf16)
        env_ref[at, FB:] = (-s[:, BAND:]).astype(bf16)

    each_block(jnp.where(lane < BAND, band(lane & (BAND - 1)), lane - BAND + 1), base, store)
    copy.wait()
    xh, core = ids[0], ids[1]
    for m in range(8):
        rows[pl.ds(128 * m, 128), :] = d_ref[:, pl.ds(128 * m, 128)].astype(f32).T

    def nodes(h, b, j):
        parts = []
        for zh in (2 * j, 2 * j + 1):
            for y in range(4):
                for xl in range(2):
                    x = 2 * (xh ^ h) + xl
                    at = pl.multiple_of((((x * 4 + zh) * 4 + y) * 2 + (core ^ b)) * 8, 8)
                    parts.append(rows[pl.ds(at, 8), :])
        return jnp.concatenate(parts, axis=0).T.astype(jnp.int32)

    for j in range(2):
        mine[j] = nodes(0, 0, j)
        far[j] = nodes(1, 0, j).astype(jnp.int16)
        for h in range(2):
            cross[h, j] = nodes(h, 1, j).astype(jnp.int16)


def split(v):
    high = v.astype(bf16).astype(f32)
    middle = (v - high).astype(bf16).astype(f32)
    return high, middle, (v - high) - middle


def times_kernel(offs, after, q_ref):
    scale = 1.0 / math.sqrt(FB * CHANNELS)
    for w in range(2):
        at = DEC * iota((16, TB), 1) + offs[w]
        low = circle((1 + iota((16, TB), 0)) * at)
        high = circle(16 * iota((16, TB), 0) * at)
        for a in range(FB // 16):
            c, s = turn([v[a : a + 1] for v in high], low)
            for i, (re, im) in enumerate(zip(split(c * scale), split(s * -scale))):
                q_ref[w, i, 16 * a : 16 * a + 16] = re.astype(bf16)
                q_ref[w, i, FB + 16 * a : FB + 16 * a + 16] = im.astype(bf16)


def inverse_kernel(after, inv_ref, base):
    _, taper = circle(2 * (band(iota((1, BAND), 1)) - BAND_LO) + 1)
    weight = taper * taper * (2.0 / SAMPLES)

    def store(at, c, s):
        store_band(inv_ref, at, weight * c, weight * s)

    each_block(band(iota((32, BAND), 1)), base, store)


def front_kernel(ids, own_ref, peer_ref, fwd_ref, inv_ref, env_ref, e_ref):
    tm = ids[2]
    own = own_ref[pl.ds(2 * tm, 2)].reshape(64, HALF)
    peer = peer_ref[...].reshape(64, HALF)
    terms = jnp.dot(jnp.concatenate([own, peer], axis=0), fwd_ref[...], preferred_element_type=f32)
    even = terms[:64, :BAND] + terms[64:, :BAND]
    odd = (terms[:64, BAND:] - terms[64:, BAND:]) * jnp.where(tm == 0, 1.0, -1.0)
    halves = []
    for i, v in enumerate((even, odd)):
        re, im = v[:, : BAND // 2], v[:, BAND // 2 :]
        forms = jnp.concatenate(
            [jnp.concatenate([re, -im], axis=1), jnp.concatenate([im, re], axis=1)], axis=0
        ).astype(bf16)
        table = inv_ref[:, BAND * i : BAND * (i + 1)]
        halves.append(lax.dot_general(forms, table, (((1,), (1,)), ((), ())), preferred_element_type=f32))
    first, second = halves[0] + halves[1], halves[0] - halves[1]
    energy = jnp.concatenate([v[:64] * v[:64] + v[64:] * v[64:] for v in (first, second)], axis=0)
    sums = jnp.sum(energy, axis=1, keepdims=True)
    sums = sums[:64] + sums[64:]
    env = jnp.dot(energy.astype(bf16), env_ref[...], preferred_element_type=f32)
    lane = lax.broadcasted_iota(jnp.int32, (1, 2 * FB), 1)
    flip_sign = (2 * (lane & 1) - 1).astype(f32)
    env = env[:64] + env[64:] * flip_sign
    factor = 1.0 / (math.sqrt(SAMPLES) * (sums / SAMPLES + epsilon))
    e_ref[...] = (env * factor).astype(bf16)


def expand(normal, lhs):
    normal = normal.astype(f32)
    kept = (iota((FB, 128), 0) & 1) == (iota((FB, 128), 1) >> 6)
    for w in range(2):
        re = normal[32 * w : 32 * w + 32, :FB]
        im = normal[32 * w : 32 * w + 32, FB:]
        for part, quad in enumerate(((re, -im, re, -im), (im, re, im, re))):
            t = jnp.concatenate(quad, axis=0).T
            lhs[pl.ds(2 * w + part, FB, stride=4), :] = jnp.where(kept, t, 0.0)


def stack(delays, lhs, store):
    one = [half_turn((d.astype(jnp.int32) - 512).astype(f32) * (math.pi / 1024)) for d in delays]
    two = [turn(v, v) for v in one]
    mid = two
    for i in range(FB // 4):
        powers, ahead = [[], [], [], []], []
        for (c, s), (c1, s1), v2 in zip(mid, one, two):
            cc, ss, cs, sc = c * c1, s * s1, c * s1, s * c1
            last = turn((c, s), v2)
            for group, v in zip(powers, ((cc + ss, sc - cs), (c, s), (cc - ss, sc + cs), last)):
                group.append([x.astype(bf16) for x in v])
            ahead.append(turn(last, v2))
        mid = ahead
        at = 16 * i
        a = jnp.concatenate([v[at : at + 16, :] for v in lhs], axis=1)
        for g in range(2):
            z = [x for even, odd in zip(powers[2 * g], powers[2 * g + 1]) for x in (*even, *odd)]
            r = jnp.dot(a, jnp.concatenate(z, axis=0), preferred_element_type=f32)
            store(at + 8 * g, r[8 * g : 8 * g + 8])


def near_kernel(own_d, core_d, own_e, core_e, acc_ref, wide, lhs):
    for i, e in enumerate((own_e, core_e)):
        expand(e[...], wide)
        lhs[i] = wide[...].astype(bf16)
    for j in range(2):

        def store(at, r):
            acc_ref[j, at : at + 8, :] = r

        stack((own_d[j], core_d[0, j]), (lhs.at[0], lhs.at[1]), store)


def far_kernel(far_d, far_e, acc_ref, out_ref, wide, lhs, acc):
    for i in range(2):
        expand(far_e[i], wide)
        lhs[i] = wide[...].astype(bf16)
    for j in range(2):

        def store(at, r):
            acc[at : at + 8, :] = acc_ref[j, at : at + 8, :] + r

        stack((far_d[0, j], far_d[1, j]), (lhs.at[0], lhs.at[1]), store)
        for q in range(4):
            out_ref[128 * j : 128 * j + 128, 128 * q : 128 * q + 128] = acc[pl.ds(q, FB, stride=4), :].T.astype(bf16)


def final_kernel(part_ref, q_ref, out_ref):
    total = part_ref[0:16, :].astype(f32)
    for i in range(1, 16):
        total = total + part_ref[16 * i : 16 * i + 16, :].astype(f32)
    total = total[:8] + total[8:]
    zero = jnp.zeros((8, TB), f32)
    for w in range(2):
        a = jnp.concatenate([*split(total[:, w * TB : (w + 1) * TB]), zero], axis=0).astype(bf16)
        r = [jnp.dot(a, q_ref[w, i], preferred_element_type=f32) for i in range(3)]
        out_ref[w] = (r[0][:8] + ((r[0][8:16] + r[1][:8]) + ((r[0][16:24] + r[1][8:16]) + r[2][:8])))


def call(kernel, outs, ins, scratch=(), limit=24):
    return pl.pallas_call(
        kernel,
        out_shape=outs,
        in_specs=ins,
        out_specs=jax.tree.map(lambda _: VMEM, outs),
        scratch_shapes=list(scratch),
        compiler_params=pltpu.CompilerParams(vmem_limit_bytes=limit << 20),
    )


def flip(v, *axes):
    n = 2 ** len(axes)
    return lax.ppermute(v, axes, [(i, n - 1 - i) for i in range(n)])


def shape(dims, dtype):
    return jax.ShapeDtypeStruct(dims, dtype)


def on_device(traces, delays, offsets):
    tm = lax.axis_index("tm")
    ids = jnp.stack([lax.axis_index(a) for a in ("xh", "core", "tm")]).astype(jnp.int32)
    rows = traces.transpose(1, 0, 2)
    send = jnp.where(tm == 0, rows[2:], rows[:2])
    peer = flip(send, "tm")
    mine, far, cross, fwd, env = call(
        first_kernel,
        (
            shape((2, 32, 128), jnp.int32),
            shape((2, 32, 128), jnp.int16),
            shape((2, 2, 32, 128), jnp.int16),
            shape((HALF, 2 * BAND), bf16),
            shape((HALF, 2 * FB), bf16),
        ),
        [SMEM, HBM, VMEM],
        [
            pltpu.VMEM((32, 1024), jnp.int32),
            pltpu.VMEM((1024, 32), f32),
            pltpu.VMEM((2, 32, BAND + FB), f32),
            pltpu.SemaphoreType.DMA,
        ],
    )(ids, pltpu.with_memory_space_constraint(delays.T, pltpu.HBM), send)
    core_d = flip(cross, "core")
    inv = call(
        inverse_kernel, shape((HALF, 2 * BAND), bf16), [VMEM], [pltpu.VMEM((2, 32, BAND), f32)]
    )(mine)
    peer, core_d, inv = lax.optimization_barrier((peer, core_d, inv))
    e = call(front_kernel, shape((64, 2 * FB), bf16), [SMEM] + [VMEM] * 5)(ids, rows, peer, fwd, inv, env)
    far_d = flip(jnp.stack([far, core_d[1]]), "xh", "xl")
    core_e = flip(e, "core")
    far_e = flip(jnp.stack([e, core_e]), "xh", "xl")
    acc = call(
        near_kernel,
        shape((2, 512, 128), f32),
        [VMEM] * 4,
        [pltpu.VMEM((512, 128), f32), pltpu.VMEM((2, 512, 128), bf16)],
    )(mine, core_d, e, core_e)
    offsets, after = lax.optimization_barrier((offsets, acc[0, :8]))
    q = call(times_kernel, shape((2, 3, 2 * FB, TB), bf16), [SMEM, VMEM])(offsets, after)
    q, acc = lax.optimization_barrier((q, acc))
    part = call(
        far_kernel,
        shape((256, 512), bf16),
        [VMEM] * 3,
        [pltpu.VMEM((512, 128), f32), pltpu.VMEM((2, 512, 128), bf16), pltpu.VMEM((512, 128), f32)],
    )(far_d, far_e, acc)
    parts = lax.all_to_all(part.reshape(32, 8, 512), ("zh", "y", "xl"), 0, 0, tiled=True)
    return call(final_kernel, shape((2, 8, TB), f32), [VMEM] * 2)(parts.reshape(256, 512), q)


def solution(mesh):
    chan = ("xh", "xl", "zh", "y", "core")
    fine = Mesh(mesh.devices.reshape(2, 2, 4, 4, 2, 2), chan + ("tm",))
    placed = (P(chan, None, "tm"), P(None, chan), P("tm"))
    return jax.shard_map(
        on_device, mesh=fine, in_specs=placed, out_specs=P("tm", chan, None), check_vma=False
    )
```
